512 devices in a mesh: dp: 16 (over x_hi, y, core), factor: 32 (over x_lo, z).
Axes of the slice: x: 4 (x_hi: 2, x_lo: 2; x = x_hi * 2 + x_lo), y: 4, z: 16, core: 2. Of those that a mesh axis runs over, the one named last changes fastest.
Arguments:
- activations: bfloat16 [2048, 8192], P('dp', 'factor'), may hold values from -12 to 12
- gradients: bfloat16 [2048, 8192], P('dp', 'factor'), may hold values from -12 to 12
- act_basis: bfloat16 [8192, 8192], P('dp', 'factor'), may hold values from -0.0625 to 0.0625
- grad_basis: bfloat16 [8192, 8192], P('dp', 'factor'), may hold values from -0.0625 to 0.0625
Outputs:
- corrected: float32 [8192, 8192], P('factor', 'dp')
The draws below stay inside these ranges and needn't reach their ends.
All inputs are finite; a program needn't handle non-finite values.
Results may differ from the reference program's by a relative error of at most 0.00062.
Values may be sent and summed in bfloat16 or wider, within the bound.
No kernel may reach another device: no remote copies, remote signals or barrier semaphores. Data moves between devices by JAX's collectives and lax.ppermute only.
A program may use at most 64 MiB of HBM per device.

```python
import math
import jax
import jax.numpy as jnp

D = 8192
LABELS = 8192
TOKENS = 2048


def token_scales(key, rows, salt):
    return jnp.exp(jax.random.uniform(jax.random.fold_in(key, salt), (rows, 1), jnp.float32, math.log(0.3), math.log(3.0)))


def scaled_rows(key, rows, width, salt):
    scales = token_scales(key, rows, salt)
    inner = jax.random.fold_in(key, salt + 7)
    base = jnp.clip(jax.random.normal(inner, (rows, width), jnp.float32), -4.0, 4.0)
    values = base * scales
    return values.astype(jnp.bfloat16)


def draw_activations(key, part):
    return scaled_rows(key, TOKENS, D, 11)


def draw_gradients(key, part):
    return scaled_rows(key, TOKENS, LABELS, 23)


def shard_levels(own_key, extent, cuts, low, high):
    def one(position, blocks):
        heights = jax.random.uniform(jax.random.fold_in(jax.random.fold_in(own_key, 6), position), (blocks,), jnp.float32, low / len(cuts), high / len(cuts))
        return jnp.repeat(jnp.exp(heights), extent[position] // blocks).reshape((-1,) + (1,) * (len(extent) - position - 1))

    gain = one(*cuts[0])
    for cut in cuts[1:]:
        gain = gain * one(*cut)
    return gain


def gaussian(stream_key, extent, scale, most, cuts=(), held_as=jnp.bfloat16):
    loudness = shard_levels(stream_key, extent, cuts, -0.22, 0.18) if cuts else 1.0
    array = jax.random.normal(stream_key, extent, jnp.float32) * scale * loudness
    return jnp.minimum(jnp.maximum(array, -most), most).astype(held_as)


def setup_inputs(seed: int = 0) -> dict:
    key_list = jax.random.split(jax.random.key(seed), 5)
    return {
        "activations": draw_activations(jax.random.fold_in(key_list[4], 71), 0),
        "gradients": draw_gradients(jax.random.fold_in(key_list[4], 71), 0),
        "act_basis": gaussian(key_list[2], (D, D), D ** -0.5, 0.0625, ((0, 16), (1, 32))),
        "grad_basis": gaussian(key_list[3], (LABELS, LABELS), LABELS ** -0.5, 0.0625, ((0, 16), (1, 32))),
    }


def reference(activations, gradients, act_basis, grad_basis):
    rotated_act = jnp.dot(activations.astype(jnp.float32), act_basis.astype(jnp.float32), preferred_element_type=jnp.float32)
    act_square = (rotated_act * rotated_act).astype(jnp.bfloat16)
    rotated_grad = jnp.dot(gradients.astype(jnp.float32), grad_basis.astype(jnp.float32), preferred_element_type=jnp.float32)
    grad_square = (rotated_grad * rotated_grad).astype(jnp.bfloat16)
    total = jnp.dot(act_square.astype(jnp.float32).T, grad_square.astype(jnp.float32), preferred_element_type=jnp.float32)
    return total * (1.0 / TOKENS)
```

```python
import functools
import jax
import jax.numpy as jnp
from jax import lax
from jax.experimental import pallas as pl
from jax.experimental.pallas import tpu as pltpu
from jax.sharding import Mesh, PartitionSpec as P

AXES = ("xh", "y", "c", "xl", "zh", "zl")
SIZES = (2, 4, 2, 2, 4, 4)
VMEM = pl.BlockSpec(memory_space=pltpu.VMEM)
SMEM = pl.BlockSpec(memory_space=pltpu.SMEM)
PARAMS = pltpu.CompilerParams(vmem_limit_bytes=40 * 1024 * 1024)


def to_all(x, axes, n):
    spread = jnp.broadcast_to(x[None], (n,) + x.shape)
    return lax.all_to_all(spread, axes, split_axis=0, concat_axis=0, tiled=True)


def move(x, axes, target):
    sizes = [SIZES[AXES.index(a)] for a in axes]

    def flat(coords):
        out = 0
        for c, s in zip(coords, sizes):
            out = out * s + c
        return out

    total = 1
    for s in sizes:
        total *= s
    pairs = []
    for i in range(total):
        rest, coords = i, []
        for s in reversed(sizes):
            coords.insert(0, rest % s)
            rest //= s
        pairs.append((i, flat(target(*coords))))
    return lax.ppermute(x, axes, pairs)


def dot(a, b):
    return jnp.dot(a, b, preferred_element_type=jnp.float32)


def grad_kernel(at_ref, g_ref, near_ref, far_ref, near_other_ref, far_other_ref, mine_ref, theirs_ref):
    y, c, turned = at_ref[0], at_ref[1], at_ref[2]
    sums = []
    for own, other in ((near_ref, near_other_ref), (far_ref, far_other_ref)):
        acc = jnp.zeros(mine_ref.shape, jnp.float32)
        for j in range(4):
            at = 4 * lax.rem(y + 4 - j, 4)
            for h in range(2):
                rows = slice(256 * h, 256 * h + 256)
                acc += dot(g_ref[at + 2 * c + h], own[j, rows, :])
                acc += dot(g_ref[at + 2 * (1 - c) + h], other[j, rows, :])
        sums.append(acc)
    near, far = sums
    mine_ref[...] = jnp.where(turned == 0, near, far)
    theirs_ref[...] = jnp.where(turned == 0, far, near)


def act_kernel(at_ref, a_ref, near_ref, far_ref, out_ref):
    c, xl = at_ref[0], at_ref[1]
    for y in range(4):
        for basis, x in ((near_ref, xl), (far_ref, 1 - xl)):
            acc = jnp.zeros(out_ref.shape[1:], jnp.float32)
            for k, core in ((0, c), (1, 1 - c)):
                for h in range(2):
                    rows = slice(256 * h, 256 * h + 256)
                    acc += dot(a_ref[4 * y + 2 * core + h], basis[k, rows, :])
            out_ref[2 * y + x] = acc


def corrected_kernel(x_ref, r_ref, s_ref, out_ref):
    x = x_ref[0]
    for h in range(2):
        acc = jnp.zeros((256, 256), jnp.float32)
        for y in range(4):
            for c in range(2):
                acc += lax.dot_general(
                    r_ref[4 * y + 2 * x + c], s_ref[4 * y + 2 * c + h],
                    (((0,), (0,)), ((), ())), preferred_element_type=jnp.float32,
                )
        out_ref[:, 256 * h:256 * h + 256] = acc


def call(kernel, shapes, *args):
    single = not isinstance(shapes, list)
    out = pl.pallas_call(
        kernel,
        out_shape=[jax.ShapeDtypeStruct(s, jnp.float32) for s in ([shapes] if single else shapes)],
        in_specs=[SMEM] + [VMEM] * (len(args) - 1),
        out_specs=[VMEM] * (1 if single else len(shapes)),
        compiler_params=PARAMS,
    )(*args)
    return out[0] if single else out


def swap(x, axis):
    return move(x, (axis,), lambda i: (1 - i,))


def on_device(activations, gradients, act_basis, grad_basis):
    tokens = activations.shape[0] * 16
    xh, y, c, xl = (lax.axis_index(a) for a in ("xh", "y", "c", "xl"))

    grad_half = to_all(gradients, ("zh", "zl"), 16)
    act_moved = move(activations, ("xh", "y", "xl", "zh"), lambda a, b, p, q: (p, q, a, b))

    grad_basis, act_basis, act_moved = lax.optimization_barrier((grad_basis, act_basis, act_moved))
    act_every = lax.all_gather(act_moved, ("zh", "zl"), axis=0, tiled=False)
    turned = move(grad_basis, ("xh", "xl"), lambda a, b: (b, a))
    near = jnp.stack(
        [turned] + [move(turned, ("y",), lambda b, j=j: ((b + j) % 4,)) for j in (1, 2, 3)]
    )
    far = swap(near, "xh")
    near_other, far_other = swap(near, "c"), swap(far, "c")

    act_near = jnp.stack([act_basis, swap(act_basis, "c")])
    act_far = swap(act_near, "xl")

    mine, theirs = call(
        grad_kernel, [(128, 256), (128, 256)],
        jnp.stack([y, c, (xh + xl) % 2]), grad_half, near, far, near_other, far_other,
    )
    rotated_grad = mine + swap(theirs, "xl")
    grad_square = (rotated_grad * rotated_grad).astype(jnp.bfloat16)
    grad_square = move(
        grad_square, AXES, lambda a, b, e, p, q, r: (p, q, r // 2, a, b, 2 * e + r % 2)
    )

    act_every, mine = lax.optimization_barrier((act_every, mine))
    part = call(act_kernel, (8, 128, 256), jnp.stack([c, xl]), act_every, act_near, act_far)
    part = lax.all_to_all(part, ("xh", "y"), split_axis=0, concat_axis=0, tiled=True)
    rotated_act = jnp.sum(part, axis=0)
    act_square = (rotated_act * rotated_act).astype(jnp.bfloat16)
    act_block = lax.all_gather(act_square, ("xh", "y", "c"), axis=0, tiled=False)
    grad_block = to_all(grad_square, ("zh", "zl"), 16)

    theirs = call(corrected_kernel, (256, 512), (1 - xl)[None], act_block, grad_block)
    theirs = swap(theirs, "xl")
    mine = call(corrected_kernel, (256, 512), xl[None], act_block, grad_block)
    return (mine + theirs) * (1.0 / tokens)


def solution(mesh):
    fine = Mesh(mesh.devices.reshape(SIZES), AXES)
    spec = P(("xh", "y", "c"), ("xl", "zh", "zl"))
    return jax.shard_map(
        on_device,
        mesh=fine,
        in_specs=(spec, spec, spec, spec),
        out_specs=P(("xl", "zh", "zl"), ("xh", "y", "c")),
        check_vma=False,
    )
```

```python
import functools
import jax
import jax.numpy as jnp
from jax import lax
from jax.experimental import pallas as pl
from jax.experimental.pallas import tpu as pltpu
from jax.sharding import Mesh, PartitionSpec as P

AXES = ("xh", "y", "c", "xl", "zh", "zl")
SIZES = (2, 4, 2, 2, 4, 4)
VMEM = pl.BlockSpec(memory_space=pltpu.VMEM)
SMEM = pl.BlockSpec(memory_space=pltpu.SMEM)
PARAMS = pltpu.CompilerParams(vmem_limit_bytes=40 * 1024 * 1024)


def to_all(x, axes, n):
    spread = jnp.broadcast_to(x[None], (n,) + x.shape)
    return lax.all_to_all(spread, axes, split_axis=0, concat_axis=0, tiled=True)


def move(x, axes, target):
    sizes = [SIZES[AXES.index(a)] for a in axes]

    def flat(coords):
        out = 0
        for c, s in zip(coords, sizes):
            out = out * s + c
        return out

    total = 1
    for s in sizes:
        total *= s
    pairs = []
    for i in range(total):
        rest, coords = i, []
        for s in reversed(sizes):
            coords.insert(0, rest % s)
            rest //= s
        pairs.append((i, flat(target(*coords))))
    return lax.ppermute(x, axes, pairs)


def dot(a, b):
    return jnp.dot(a, b, preferred_element_type=jnp.float32)


def grad_kernel(at_ref, g_ref, near_ref, far_ref, near_other_ref, far_other_ref, mine_ref, theirs_ref):
    y, c, turned = at_ref[0], at_ref[1], at_ref[2]
    sums = []
    for own, other in ((near_ref, near_other_ref), (far_ref, far_other_ref)):
        acc = jnp.zeros(mine_ref.shape, jnp.float32)
        for j in range(4):
            at = 4 * lax.rem(y + 4 - j, 4)
            for h in range(2):
                rows = slice(256 * h, 256 * h + 256)
                acc += dot(g_ref[at + 2 * c + h, 1], own[j, rows, :])
                acc += dot(g_ref[at + 2 * (1 - c) + h, 1], other[j, rows, :])
        sums.append(acc)
    near, far = sums
    mine_ref[...] = jnp.where(turned == 0, near, far)
    theirs_ref[...] = jnp.where(turned == 0, far, near)


def act_kernel(at_ref, a_ref, near_ref, far_ref, out_ref):
    c, xl = at_ref[0], at_ref[1]
    for y in range(4):
        for basis, x in ((near_ref, xl), (far_ref, 1 - xl)):
            acc = jnp.zeros(out_ref.shape[1:], jnp.float32)
            for k, core in ((0, c), (1, 1 - c)):
                for h in range(2):
                    rows = slice(256 * h, 256 * h + 256)
                    acc += dot(a_ref[4 * y + 2 * core + h, 0], basis[k, rows, :])
            out_ref[2 * y + x] = acc


def corrected_kernel(at_ref, near_ref, far_ref, s_ref, out_ref):
    x, xh, y, c = at_ref[0], at_ref[1], at_ref[2], at_ref[3]
    for h in range(2):
        acc = jnp.zeros((256, 256), jnp.float32)
        for act, high in ((near_ref, xh), (far_ref, 1 - xh)):
            for low in range(2):
                shift = lax.rem(y + 4 - x - 2 * low, 4)
                for k, core in ((0, c), (1, 1 - c)):
                    acc += lax.dot_general(
                        act[2 * shift + k], s_ref[8 * high + 4 * low + 2 * core + h],
                        (((0,), (0,)), ((), ())), preferred_element_type=jnp.float32,
                    )
        out_ref[:, 256 * h:256 * h + 256] = acc


def call(kernel, shapes, *args):
    single = not isinstance(shapes, list)
    out = pl.pallas_call(
        kernel,
        out_shape=[jax.ShapeDtypeStruct(s, jnp.float32) for s in ([shapes] if single else shapes)],
        in_specs=[SMEM] + [VMEM] * (len(args) - 1),
        out_specs=[VMEM] * (1 if single else len(shapes)),
        compiler_params=PARAMS,
    )(*args)
    return out[0] if single else out


def swap(x, axis):
    return move(x, (axis,), lambda i: (1 - i,))


def shift_y(x, j):
    return move(x, ("y",), lambda b: ((b + j) % 4,))


def on_device(activations, gradients, act_basis, grad_basis):
    tokens = activations.shape[0] * 16
    xh, y, c, xl = (lax.axis_index(a) for a in ("xh", "y", "c", "xl"))

    act_moved = move(activations, ("xh", "y", "xl", "zh"), lambda a, b, p, q: (p, q, a, b))
    both = jnp.stack([act_moved, gradients])
    both, grad_basis, act_basis = lax.optimization_barrier((both, grad_basis, act_basis))
    every = lax.all_gather(both, ("zh", "zl"), axis=0, tiled=False)

    turned = move(grad_basis, ("xh", "xl"), lambda a, b: (b, a))
    near = jnp.stack([turned] + [shift_y(turned, j) for j in (1, 2, 3)])
    far = swap(near, "xh")
    near_other, far_other = swap(near, "c"), swap(far, "c")

    act_near = jnp.stack([act_basis, swap(act_basis, "c")])
    act_far = swap(act_near, "xl")

    mine, theirs = call(
        grad_kernel, [(128, 256), (128, 256)],
        jnp.stack([y, c, (xh + xl) % 2]), every, near, far, near_other, far_other,
    )
    rotated_grad = mine + swap(theirs, "xl")
    grad_square = (rotated_grad * rotated_grad).astype(jnp.bfloat16)
    grad_square = move(
        grad_square, AXES, lambda a, b, e, p, q, r: (p, q, r // 2, a, b, 2 * e + r % 2)
    )

    every, mine = lax.optimization_barrier((every, mine))
    part = call(act_kernel, (8, 128, 256), jnp.stack([c, xl]), every, act_near, act_far)
    part = lax.all_to_all(part, ("xh", "y"), split_axis=0, concat_axis=0, tiled=True)
    rotated_act = jnp.sum(part, axis=0)
    act_square = (rotated_act * rotated_act).astype(jnp.bfloat16)
    grad_square, act_square = lax.optimization_barrier((grad_square, act_square))
    grad_block = to_all(grad_square, ("zh", "zl"), 16)

    pair = jnp.stack([act_square, swap(act_square, "c")])
    near = jnp.concatenate([pair] + [shift_y(pair, j) for j in (1, 2, 3)])
    far = swap(near, "xh")

    theirs = call(corrected_kernel, (256, 512), jnp.stack([1 - xl, xh, y, c]), near, far, grad_block)
    theirs = swap(theirs, "xl")
    mine = call(corrected_kernel, (256, 512), jnp.stack([xl, xh, y, c]), near, far, grad_block)
    return (mine + theirs) * (1.0 / tokens)


def solution(mesh):
    fine = Mesh(mesh.devices.reshape(SIZES), AXES)
    spec = P(("xh", "y", "c"), ("xl", "zh", "zl"))
    return jax.shard_map(
        on_device,
        mesh=fine,
        in_specs=(spec, spec, spec, spec),
        out_specs=P(("xl", "zh", "zl"), ("xh", "y", "c")),
        check_vma=False,
    )
```

```python
import functools
import jax
import jax.numpy as jnp
from jax import lax
from jax.experimental import pallas as pl
from jax.experimental.pallas import tpu as pltpu
from jax.sharding import Mesh, PartitionSpec as P

AXES = ("xh", "y", "c", "xl", "zh", "zl")
SIZES = (2, 4, 2, 2, 4, 4)
VMEM = pl.BlockSpec(memory_space=pltpu.VMEM)
SMEM = pl.BlockSpec(memory_space=pltpu.SMEM)
PARAMS = pltpu.CompilerParams(vmem_limit_bytes=40 * 1024 * 1024)


def to_all(x, axes, n):
    spread = jnp.broadcast_to(x[None], (n,) + x.shape)
    return lax.all_to_all(spread, axes, split_axis=0, concat_axis=0, tiled=True)


def move(x, axes, target):
    sizes = [SIZES[AXES.index(a)] for a in axes]

    def flat(coords):
        out = 0
        for c, s in zip(coords, sizes):
            out = out * s + c
        return out

    total = 1
    for s in sizes:
        total *= s
    pairs = []
    for i in range(total):
        rest, coords = i, []
        for s in reversed(sizes):
            coords.insert(0, rest % s)
            rest //= s
        pairs.append((i, flat(target(*coords))))
    return lax.ppermute(x, axes, pairs)


def dot(a, b):
    return jnp.dot(a, b, preferred_element_type=jnp.float32)


def rotate_kernel(at_ref, x_ref, near_ref, far_ref, near_other_ref, far_other_ref, mine_ref, theirs_ref):
    y, c, turned = at_ref[0], at_ref[1], at_ref[2]
    sums = []
    for own, other in ((near_ref, near_other_ref), (far_ref, far_other_ref)):
        acc = jnp.zeros(mine_ref.shape, jnp.float32)
        for j in range(4):
            at = 4 * lax.rem(y + 4 - j, 4)
            for h in range(2):
                rows = slice(256 * h, 256 * h + 256)
                acc += dot(x_ref[at + 2 * c + h, 0], own[j, 0, rows, :])
                acc += dot(x_ref[at + 2 * (1 - c) + h, 0], other[j, 0, rows, :])
        sums.append(acc)
    near, far = sums
    mine_ref[...] = jnp.where(turned == 0, near, far)
    theirs_ref[...] = jnp.where(turned == 0, far, near)


def corrected_kernel(at_ref, near_ref, far_ref, near_other_ref, far_other_ref, s_ref, out_ref):
    y, c, which = at_ref[0], at_ref[1], at_ref[2]

    def contract(own, other):
        for h in range(2):
            acc = jnp.zeros((256, 256), jnp.float32)
            for j in range(4):
                at = 4 * lax.rem(y + 4 - j, 4) + h
                for act, core in ((own, c), (other, 1 - c)):
                    acc += lax.dot_general(
                        act[j], s_ref[at + 2 * core],
                        (((0,), (0,)), ((), ())), preferred_element_type=jnp.float32,
                    )
            out_ref[:, 256 * h:256 * h + 256] = acc

    @pl.when(which == 0)
    def _():
        contract(near_ref, near_other_ref)

    @pl.when(which != 0)
    def _():
        contract(far_ref, far_other_ref)


def rotate(at, x, part, bases, basis_part):
    one = lambda shape, part: pl.BlockSpec(
        (shape[0], 1) + shape[2:], lambda i: (0, part, 0, 0), pipeline_mode=pl.Buffered(1)
    )
    out = jax.ShapeDtypeStruct(x.shape[2:], jnp.float32)
    return pl.pallas_call(
        rotate_kernel,
        grid=(1,),
        out_shape=[out, out],
        in_specs=[SMEM, one(x.shape, part)] + [one(b.shape, basis_part) for b in bases],
        out_specs=[pl.BlockSpec(out.shape, lambda i: (0, 0))] * 2,
        compiler_params=PARAMS,
    )(at, x, *bases)


def correct(at, acts, grads):
    return pl.pallas_call(
        corrected_kernel,
        out_shape=jax.ShapeDtypeStruct((256, 512), jnp.float32),
        in_specs=[SMEM] + [VMEM] * 5,
        out_specs=VMEM,
        compiler_params=PARAMS,
    )(at, *acts, grads)


def swap(x, axis):
    return move(x, (axis,), lambda i: (1 - i,))


def plane_gather(x):
    own = []
    for k in range(2):
        blocks = [
            move(x, ("xh", "y", "xl"), lambda a, b, p, j=j: (p ^ k, (b + j) % 4, a)) for j in range(4)
        ]
        own.append(jnp.stack(blocks))
    return own + [swap(o, "c") for o in own]


def square(mine, theirs):
    total = mine + swap(theirs, "xl")
    return (total * total).astype(jnp.bfloat16)


def on_device(activations, gradients, act_basis, grad_basis):
    tokens = activations.shape[0] * 16
    xh, y, c, xl = (lax.axis_index(a) for a in ("xh", "y", "c", "xl"))
    turned = (xh + xl) % 2
    at = jnp.stack([y, c, turned])

    both = jnp.stack([activations, gradients])
    act_every = grad_every = lax.all_gather(both, ("zh", "zl"), axis=0, tiled=False)
    bases = plane_gather(jnp.stack([act_basis, grad_basis]))

    mine, theirs = rotate(at, grad_every, 1, bases, 1)
    grad_square = square(mine, theirs)
    grad_square = move(
        grad_square, AXES, lambda a, b, e, p, q, r: (p, q, r // 2, a, b, 2 * e + r % 2)
    )

    act_every, mine = lax.optimization_barrier((act_every, mine))
    act_square = square(*rotate(at, act_every, 0, bases, 0))
    grad_square, act_square = lax.optimization_barrier((grad_square, act_square))
    grad_block = to_all(grad_square, ("zh", "zl"), 16)
    acts = plane_gather(act_square)

    theirs = swap(correct(jnp.stack([y, c, 1 - turned]), acts, grad_block), "xl")
    mine = correct(at, acts, grad_block)
    return (mine + theirs) * (1.0 / tokens)


def solution(mesh):
    fine = Mesh(mesh.devices.reshape(SIZES), AXES)
    spec = P(("xh", "y", "c"), ("xl", "zh", "zl"))
    return jax.shard_map(
        on_device,
        mesh=fine,
        in_specs=(spec, spec, spec, spec),
        out_specs=P(("xl", "zh", "zl"), ("xh", "y", "c")),
        check_vma=False,
    )
```

```python
import functools
import jax
import jax.numpy as jnp
from jax import lax
from jax.experimental import pallas as pl
from jax.experimental.pallas import tpu as pltpu
from jax.sharding import Mesh, PartitionSpec as P

AXES = ("xh", "y", "c", "xl", "zh", "zl")
SIZES = (2, 4, 2, 2, 4, 4)
VMEM = pl.BlockSpec(memory_space=pltpu.VMEM)
SMEM = pl.BlockSpec(memory_space=pltpu.SMEM)
PARAMS = pltpu.CompilerParams(vmem_limit_bytes=40 * 1024 * 1024)


def to_all(x, axes, n):
    spread = jnp.broadcast_to(x[None], (n,) + x.shape)
    return lax.all_to_all(spread, axes, split_axis=0, concat_axis=0, tiled=True)


def move(x, axes, target):
    sizes = [SIZES[AXES.index(a)] for a in axes]

    def flat(coords):
        out = 0
        for c, s in zip(coords, sizes):
            out = out * s + c
        return out

    total = 1
    for s in sizes:
        total *= s
    pairs = []
    for i in range(total):
        rest, coords = i, []
        for s in reversed(sizes):
            coords.insert(0, rest % s)
            rest //= s
        pairs.append((i, flat(target(*coords))))
    return lax.ppermute(x, axes, pairs)


def dot(a, b):
    return jnp.dot(a, b, preferred_element_type=jnp.float32)


def rotate_kernel(at_ref, x_ref, own_ref, other_ref, mine_ref, theirs_ref):
    y, c, turned = at_ref[0], at_ref[1], at_ref[2]
    sums = []
    for k in range(2):
        acc = jnp.zeros(mine_ref.shape, jnp.float32)
        for j in range(4):
            at = 4 * lax.rem(y + 4 - j, 4)
            for h in range(2):
                rows = slice(256 * h, 256 * h + 256)
                acc += dot(x_ref[at + 2 * c + h, 0], own_ref[j, k, rows, :])
                acc += dot(x_ref[at + 2 * (1 - c) + h, 0], other_ref[j, k, rows, :])
        sums.append(acc)
    near, far = sums
    mine_ref[...] = jnp.where(turned == 0, near, far)
    theirs_ref[...] = jnp.where(turned == 0, far, near)


def corrected_kernel(at_ref, own_ref, other_ref, s_ref, out_ref):
    y, c, k = at_ref[0], at_ref[1], at_ref[2]
    for h in range(2):
        acc = jnp.zeros((256, 256), jnp.float32)
        for j in range(4):
            at = 4 * lax.rem(y + 4 - j, 4) + h
            for act, core in ((own_ref, c), (other_ref, 1 - c)):
                acc += lax.dot_general(
                    act[j, k], s_ref[at + 2 * core],
                    (((0,), (0,)), ((), ())), preferred_element_type=jnp.float32,
                )
        out_ref[:, 256 * h:256 * h + 256] = acc


def rotate(at, x, part, basis):
    out = jax.ShapeDtypeStruct(x.shape[2:], jnp.float32)
    return pl.pallas_call(
        rotate_kernel,
        grid=(1,),
        out_shape=[out, out],
        in_specs=[SMEM, pl.BlockSpec((16, 1) + out.shape, lambda i: (0, part, 0, 0)), VMEM, VMEM],
        out_specs=[VMEM, VMEM],
        compiler_params=PARAMS,
    )(at, x, *basis)


def correct(at, acts, grads):
    return pl.pallas_call(
        corrected_kernel,
        out_shape=jax.ShapeDtypeStruct((256, 512), jnp.float32),
        in_specs=[SMEM] + [VMEM] * 3,
        out_specs=VMEM,
        compiler_params=PARAMS,
    )(at, *acts, grads)


def swap(x, axis):
    return move(x, (axis,), lambda i: (1 - i,))


def plane_gather(x):
    pair = jnp.stack([move(x, ("xh", "xl"), lambda a, p, k=k: (p ^ k, a)) for k in range(2)])
    shifted = [move(pair, ("y",), lambda b, j=j: ((b + j) % 4,)) for j in (1, 2, 3)]
    own = jnp.stack([pair] + shifted)
    return own, swap(own, "c")


def square(mine, theirs):
    total = mine + swap(theirs, "xl")
    return (total * total).astype(jnp.bfloat16)


def on_device(activations, gradients, act_basis, grad_basis):
    tokens = activations.shape[0] * 16
    xh, y, c, xl = (lax.axis_index(a) for a in ("xh", "y", "c", "xl"))
    turned = (xh + xl) % 2
    at = jnp.stack([y, c, turned])

    both = jnp.stack([activations, gradients])
    both, grad_basis = lax.optimization_barrier((both, grad_basis))
    act_every = grad_every = lax.all_gather(both, ("zh", "zl"), axis=0, tiled=False)
    grad_panels = plane_gather(grad_basis)
    act_basis, grad_own = lax.optimization_barrier((act_basis, grad_panels[0]))
    act_panels = plane_gather(act_basis)

    mine, theirs = rotate(at, grad_every, 1, grad_panels)
    grad_square = square(mine, theirs)
    grad_square = move(
        grad_square, AXES, lambda a, b, e, p, q, r: (p, q, r // 2, a, b, 2 * e + r % 2)
    )

    act_every, mine = lax.optimization_barrier((act_every, mine))
    act_square = square(*rotate(at, act_every, 0, act_panels))
    act_square, grad_square = lax.optimization_barrier((act_square, grad_square))
    grad_block = to_all(grad_square, ("zh", "zl"), 16)
    acts = plane_gather(act_square)

    theirs = swap(correct(jnp.stack([y, c, 1 - turned]), acts, grad_block), "xl")
    mine = correct(at, acts, grad_block)
    return (mine + theirs) * (1.0 / tokens)


def solution(mesh):
    fine = Mesh(mesh.devices.reshape(SIZES), AXES)
    spec = P(("xh", "y", "c"), ("xl", "zh", "zl"))
    return jax.shard_map(
        on_device,
        mesh=fine,
        in_specs=(spec, spec, spec, spec),
        out_specs=P(("xl", "zh", "zl"), ("xh", "y", "c")),
        check_vma=False,
    )
```

```python
import functools
import jax
import jax.numpy as jnp
from jax import lax
from jax.experimental import pallas as pl
from jax.experimental.pallas import tpu as pltpu
from jax.sharding import Mesh, PartitionSpec as P

AXES = ("xh", "y", "c", "xl", "zh", "zl")
SIZES = (2, 4, 2, 2, 4, 4)
VMEM = pl.BlockSpec(memory_space=pltpu.VMEM)
SMEM = pl.BlockSpec(memory_space=pltpu.SMEM)
PARAMS = pltpu.CompilerParams(vmem_limit_bytes=40 * 1024 * 1024)


def to_all(x, axes, n):
    spread = jnp.broadcast_to(x[None], (n,) + x.shape)
    return lax.all_to_all(spread, axes, split_axis=0, concat_axis=0, tiled=True)


def move(x, axes, target):
    sizes = [SIZES[AXES.index(a)] for a in axes]

    def flat(coords):
        out = 0
        for c, s in zip(coords, sizes):
            out = out * s + c
        return out

    total = 1
    for s in sizes:
        total *= s
    pairs = []
    for i in range(total):
        rest, coords = i, []
        for s in reversed(sizes):
            coords.insert(0, rest % s)
            rest //= s
        pairs.append((i, flat(target(*coords))))
    return lax.ppermute(x, axes, pairs)


def dot(a, b):
    return jnp.dot(a, b, preferred_element_type=jnp.float32)


def rotate_kernel(at_ref, x_ref, own_ref, other_ref, mine_ref, theirs_ref):
    y, c, turned = at_ref[0], at_ref[1], at_ref[2]
    sums = []
    for k in range(2):
        acc = jnp.zeros(mine_ref.shape, jnp.float32)
        for j in range(4):
            at = 4 * lax.rem(y + 4 - j, 4)
            for h in range(2):
                rows = slice(256 * h, 256 * h + 256)
                acc += dot(x_ref[at + 2 * c + h, 0], own_ref[j, k, rows, :])
                acc += dot(x_ref[at + 2 * (1 - c) + h, 0], other_ref[j, k, rows, :])
        sums.append(acc)
    near, far = sums
    mine_ref[...] = jnp.where(turned == 0, near, far)
    theirs_ref[...] = jnp.where(turned == 0, far, near)


def corrected_kernel(at_ref, own_ref, other_ref, s_ref, out_ref):
    y, c, k = at_ref[0], at_ref[1], at_ref[2]
    for h in range(2):
        acc = jnp.zeros((256, 256), jnp.float32)
        for j in range(4):
            at = 4 * lax.rem(y + 4 - j, 4) + h
            for act, core in ((own_ref, c), (other_ref, 1 - c)):
                acc += lax.dot_general(
                    act[j, k], s_ref[at + 2 * core],
                    (((0,), (0,)), ((), ())), preferred_element_type=jnp.float32,
                )
        out_ref[:, 256 * h:256 * h + 256] = acc


def rotate(at, x, part, basis):
    out = jax.ShapeDtypeStruct(x.shape[2:], jnp.float32)
    return pl.pallas_call(
        rotate_kernel,
        grid=(1,),
        out_shape=[out, out],
        in_specs=[SMEM, pl.BlockSpec((16, 1) + out.shape, lambda i: (0, part, 0, 0)), VMEM, VMEM],
        out_specs=[VMEM, VMEM],
        compiler_params=PARAMS,
    )(at, x, *basis)


def correct(at, acts, grads):
    return pl.pallas_call(
        corrected_kernel,
        out_shape=jax.ShapeDtypeStruct((256, 512), jnp.float32),
        in_specs=[SMEM] + [VMEM] * 3,
        out_specs=VMEM,
        compiler_params=PARAMS,
    )(at, *acts, grads)


def swap(x, axis):
    return move(x, (axis,), lambda i: (1 - i,))


def cross(x):
    return jnp.stack([move(x, ("xh", "xl"), lambda a, p, k=k: (p ^ k, a)) for k in range(2)])


def shifts(pair):
    return [pair] + [move(pair, ("y",), lambda b, j=j: ((b + j) % 4,)) for j in (1, 2, 3)]


def both_cores(blocks):
    own = jnp.stack(blocks)
    return own, swap(own, "c")


def square(mine, theirs):
    total = mine + swap(theirs, "xl")
    return (total * total).astype(jnp.bfloat16)


def on_device(activations, gradients, act_basis, grad_basis):
    tokens = activations.shape[0] * 16
    xh, y, c, xl = (lax.axis_index(a) for a in ("xh", "y", "c", "xl"))
    turned = (xh + xl) % 2
    at = jnp.stack([y, c, turned])

    both = jnp.stack([activations, gradients])
    both, grad_basis = lax.optimization_barrier((both, grad_basis))
    every = lax.all_gather(both, ("zh", "zl"), axis=0, tiled=False)
    grad_pair = cross(grad_basis)
    act_basis, grad_pair = lax.optimization_barrier((act_basis, grad_pair))
    grad_panels = both_cores(shifts(grad_pair))
    act_pair, grad_own = lax.optimization_barrier((cross(act_basis), grad_panels[0]))
    act_shifts = shifts(act_pair)

    mine, theirs = rotate(at, every, 1, grad_panels)
    act_shifts, mine = lax.optimization_barrier((act_shifts, mine))
    grad_square = square(mine, theirs)
    grad_square = move(
        grad_square, AXES, lambda a, b, e, p, q, r: (p, q, r // 2, a, b, 2 * e + r % 2)
    )
    grad_block = to_all(grad_square, ("zh", "zl"), 16)

    act_panels = both_cores(act_shifts)
    act_square = square(*rotate(at, every, 0, act_panels))
    acts = both_cores(shifts(cross(act_square)))

    theirs = swap(correct(jnp.stack([y, c, 1 - turned]), acts, grad_block), "xl")
    mine = correct(at, acts, grad_block)
    return (mine + theirs) * (1.0 / tokens)


def solution(mesh):
    fine = Mesh(mesh.devices.reshape(SIZES), AXES)
    spec = P(("xh", "y", "c"), ("xl", "zh", "zl"))
    return jax.shard_map(
        on_device,
        mesh=fine,
        in_specs=(spec, spec, spec, spec),
        out_specs=P(("xl", "zh", "zl"), ("xh", "y", "c")),
        check_vma=False,
    )
```

```python
import functools
import jax
import jax.numpy as jnp
from jax import lax
from jax.experimental import pallas as pl
from jax.experimental.pallas import tpu as pltpu
from jax.sharding import Mesh, PartitionSpec as P

AXES = ("xh", "y", "c", "xl", "zh", "zl")
SIZES = (2, 4, 2, 2, 4, 4)
VMEM = pl.BlockSpec(memory_space=pltpu.VMEM)
SMEM = pl.BlockSpec(memory_space=pltpu.SMEM)
PARAMS = pltpu.CompilerParams(vmem_limit_bytes=40 * 1024 * 1024)


def to_all(x, axes, n):
    spread = jnp.broadcast_to(x[None], (n,) + x.shape)
    return lax.all_to_all(spread, axes, split_axis=0, concat_axis=0, tiled=True)


def move(x, axes, target):
    sizes = [SIZES[AXES.index(a)] for a in axes]

    def flat(coords):
        out = 0
        for c, s in zip(coords, sizes):
            out = out * s + c
        return out

    total = 1
    for s in sizes:
        total *= s
    pairs = []
    for i in range(total):
        rest, coords = i, []
        for s in reversed(sizes):
            coords.insert(0, rest % s)
            rest //= s
        pairs.append((i, flat(target(*coords))))
    return lax.ppermute(x, axes, pairs)


def dot(a, b):
    return jnp.dot(a, b, preferred_element_type=jnp.float32)


def rotate_kernel(at_ref, x_ref, own_ref, other_ref, first_ref, second_ref):
    y, c, turned = at_ref[0], at_ref[1], at_ref[2]
    sums = []
    for k in range(2):
        acc = jnp.zeros(x_ref.shape[2:], jnp.float32)
        for j in range(4):
            at = 4 * lax.rem(y + 4 - j, 4)
            for h in range(2):
                rows = slice(256 * h, 256 * h + 256)
                acc += dot(x_ref[at + 2 * c + h, 0], own_ref[j, k, rows, :])
                acc += dot(x_ref[at + 2 * (1 - c) + h, 0], other_ref[j, k, rows, :])
        sums.append(acc)
    near, far = sums
    mine, theirs = jnp.where(turned == 0, near, far), jnp.where(turned == 0, far, near)
    if len(first_ref.shape) == 2:
        first_ref[...], second_ref[...] = mine, theirs
    else:
        first_ref[0], first_ref[1] = mine, theirs
        second_ref[0], second_ref[1] = theirs, mine


def corrected_kernel(at_ref, own_ref, other_ref, s_ref, out_ref):
    y, c, k = at_ref[0], at_ref[1], at_ref[2]
    for h in range(2):
        acc = jnp.zeros((256, 256), jnp.float32)
        for j in range(4):
            at = 4 * lax.rem(y + 4 - j, 4) + h
            for act, core in ((own_ref, c), (other_ref, 1 - c)):
                acc += lax.dot_general(
                    act[j, k], s_ref[at + 2 * core],
                    (((0,), (0,)), ((), ())), preferred_element_type=jnp.float32,
                )
        out_ref[:, 256 * h:256 * h + 256] = acc


def rotate(at, x, part, basis, paired):
    out = jax.ShapeDtypeStruct((2,) * paired + x.shape[2:], jnp.float32)
    return pl.pallas_call(
        rotate_kernel,
        grid=(1,),
        out_shape=[out, out],
        in_specs=[SMEM, pl.BlockSpec((16, 1) + x.shape[2:], lambda i: (0, part, 0, 0)), VMEM, VMEM],
        out_specs=[VMEM, VMEM],
        compiler_params=PARAMS,
    )(at, x, *basis)


def correct(at, acts, grads):
    return pl.pallas_call(
        corrected_kernel,
        out_shape=jax.ShapeDtypeStruct((256, 512), jnp.float32),
        in_specs=[SMEM] + [VMEM] * 3,
        out_specs=VMEM,
        compiler_params=PARAMS,
    )(at, *acts, grads)


def swap(x, axis):
    return move(x, (axis,), lambda i: (1 - i,))


def cross(x):
    return jnp.stack([move(x, ("xh", "xl"), lambda a, p, k=k: (p ^ k, a)) for k in range(2)])


def shifts(pair):
    return [pair] + [move(pair, ("y",), lambda b, j=j: ((b + j) % 4,)) for j in (1, 2, 3)]


def both_cores(blocks):
    own = jnp.stack(blocks)
    return own, swap(own, "c")


def on_device(activations, gradients, act_basis, grad_basis):
    tokens = activations.shape[0] * 16
    xh, y, c, xl = (lax.axis_index(a) for a in ("xh", "y", "c", "xl"))
    turned = (xh + xl) % 2
    at = jnp.stack([y, c, turned])

    both = jnp.stack([activations, gradients])
    both, grad_basis = lax.optimization_barrier((both, grad_basis))
    every = lax.all_gather(both, ("zh", "zl"), axis=0, tiled=False)
    grad_pair = cross(grad_basis)
    act_basis, grad_pair = lax.optimization_barrier((act_basis, grad_pair))
    grad_shifts, act_pair = lax.optimization_barrier((shifts(grad_pair), cross(act_basis)))
    grad_panels = both_cores(grad_shifts)
    act_pair, grad_own = lax.optimization_barrier((act_pair, grad_panels[0]))
    act_shifts = shifts(act_pair)

    mine, theirs = rotate(at, every, 1, grad_panels, 0)
    rotated_grad = mine + swap(theirs, "xl")
    grad_square = (rotated_grad * rotated_grad).astype(jnp.bfloat16)
    act_shifts, grad_square = lax.optimization_barrier((act_shifts, grad_square))
    grad_square = move(
        grad_square, AXES, lambda a, b, e, p, q, r: (p, q, r // 2, a, b, 2 * e + r % 2)
    )

    parts = rotate(at, every, 0, both_cores(act_shifts), 1)
    grad_square, parts = lax.optimization_barrier((grad_square, parts))
    grad_block = to_all(grad_square, ("zh", "zl"), 16)
    parts = [move(parts[k], ("xh", "xl"), lambda a, p, k=k: (p ^ k, a)) for k in range(2)]
    rotated_act = parts[0] + parts[1]
    act_square = (rotated_act * rotated_act).astype(jnp.bfloat16)
    acts = both_cores(shifts(act_square))

    theirs = swap(correct(jnp.stack([y, c, 1 - turned]), acts, grad_block), "xl")
    mine = correct(at, acts, grad_block)
    return (mine + theirs) * (1.0 / tokens)


def solution(mesh):
    fine = Mesh(mesh.devices.reshape(SIZES), AXES)
    spec = P(("xh", "y", "c"), ("xl", "zh", "zl"))
    return jax.shard_map(
        on_device,
        mesh=fine,
        in_specs=(spec, spec, spec, spec),
        out_specs=P(("xl", "zh", "zl"), ("xh", "y", "c")),
        check_vma=False,
    )
```

```python
import functools
import jax
import jax.numpy as jnp
from jax import lax
from jax.experimental import pallas as pl
from jax.experimental.pallas import tpu as pltpu
from jax.sharding import Mesh, PartitionSpec as P

AXES = ("xh", "y", "c", "xl", "zh", "zl")
SIZES = (2, 4, 2, 2, 4, 4)
VMEM = pl.BlockSpec(memory_space=pltpu.VMEM)
SMEM = pl.BlockSpec(memory_space=pltpu.SMEM)
PARAMS = pltpu.CompilerParams(vmem_limit_bytes=40 * 1024 * 1024)


def to_all(x, axes, n):
    spread = jnp.broadcast_to(x[None], (n,) + x.shape)
    return lax.all_to_all(spread, axes, split_axis=0, concat_axis=0, tiled=True)


def move(x, axes, target):
    sizes = [SIZES[AXES.index(a)] for a in axes]

    def flat(coords):
        out = 0
        for c, s in zip(coords, sizes):
            out = out * s + c
        return out

    total = 1
    for s in sizes:
        total *= s
    pairs = []
    for i in range(total):
        rest, coords = i, []
        for s in reversed(sizes):
            coords.insert(0, rest % s)
            rest //= s
        pairs.append((i, flat(target(*coords))))
    return lax.ppermute(x, axes, pairs)


def dot(a, b):
    return jnp.dot(a, b, preferred_element_type=jnp.float32)


def rotate_kernel(at_ref, x_ref, own_ref, other_ref, first_ref, second_ref):
    y, c, turned = at_ref[0], at_ref[1], at_ref[2]
    sums = []
    for k in range(2):
        acc = jnp.zeros(x_ref.shape[2:], jnp.float32)
        for j in range(4):
            at = 4 * lax.rem(y + 4 - j, 4)
            for h in range(2):
                rows = slice(256 * h, 256 * h + 256)
                acc += dot(x_ref[at + 2 * c + h, 0], own_ref[j, k, rows, :])
                acc += dot(x_ref[at + 2 * (1 - c) + h, 0], other_ref[j, k, rows, :])
        sums.append(acc)
    near, far = sums
    mine, theirs = jnp.where(turned == 0, near, far), jnp.where(turned == 0, far, near)
    if len(first_ref.shape) == 2:
        first_ref[...], second_ref[...] = mine, theirs
    else:
        first_ref[0], first_ref[1] = mine, theirs
        second_ref[0], second_ref[1] = theirs, mine


def corrected_kernel(at_ref, own_ref, other_ref, s_ref, out_ref):
    y, c, k = at_ref[0], at_ref[1], at_ref[2]
    for h in range(2):
        acc = jnp.zeros((256, 256), jnp.float32)
        for j in range(4):
            at = lax.rem(y + 4 - j, 4) + 4 * h
            for act, core in ((own_ref, c), (other_ref, 1 - c)):
                acc += lax.dot_general(
                    act[j, k], s_ref[at + 8 * core],
                    (((0,), (0,)), ((), ())), preferred_element_type=jnp.float32,
                )
        out_ref[:, 256 * h:256 * h + 256] = acc


def rotate(at, x, part, basis, paired):
    out = jax.ShapeDtypeStruct((2,) * paired + x.shape[2:], jnp.float32)
    return pl.pallas_call(
        rotate_kernel,
        grid=(1,),
        out_shape=[out, out],
        in_specs=[SMEM, pl.BlockSpec((16, 1) + x.shape[2:], lambda i: (0, part, 0, 0)), VMEM, VMEM],
        out_specs=[VMEM, VMEM],
        compiler_params=PARAMS,
    )(at, x, *basis)


def correct(at, acts, grads):
    return pl.pallas_call(
        corrected_kernel,
        out_shape=jax.ShapeDtypeStruct((256, 512), jnp.float32),
        in_specs=[SMEM] + [VMEM] * 3,
        out_specs=VMEM,
        compiler_params=PARAMS,
    )(at, *acts, grads)


def swap(x, axis):
    return move(x, (axis,), lambda i: (1 - i,))


def cross(x):
    return jnp.stack([move(x, ("xh", "xl"), lambda a, p, k=k: (p ^ k, a)) for k in range(2)])


def shifts(pair):
    return [pair] + [move(pair, ("y",), lambda b, j=j: ((b + j) % 4,)) for j in (1, 2, 3)]


def both_cores(blocks):
    own = jnp.stack(blocks)
    return own, swap(own, "c")


def on_device(activations, gradients, act_basis, grad_basis):
    tokens = activations.shape[0] * 16
    xh, y, c, xl = (lax.axis_index(a) for a in ("xh", "y", "c", "xl"))
    turned = (xh + xl) % 2
    at = jnp.stack([y, c, turned])

    both = jnp.stack([activations, gradients])
    both, grad_basis = lax.optimization_barrier((both, grad_basis))
    every = lax.all_gather(both, ("zh", "zl"), axis=0, tiled=False)
    grad_pair = cross(grad_basis)
    act_basis, grad_pair = lax.optimization_barrier((act_basis, grad_pair))
    grad_shifts, act_pair = lax.optimization_barrier((shifts(grad_pair), cross(act_basis)))
    grad_panels = both_cores(grad_shifts)
    act_pair, grad_own = lax.optimization_barrier((act_pair, grad_panels[0]))
    act_shifts = shifts(act_pair)

    mine, theirs = rotate(at, every, 1, grad_panels, 0)
    rotated_grad = mine + swap(theirs, "xl")
    grad_square = (rotated_grad * rotated_grad).astype(jnp.bfloat16)
    act_shifts, grad_square = lax.optimization_barrier((act_shifts, grad_square))
    grad_square = move(
        grad_square, AXES, lambda a, b, e, p, q, r: (p, q, r // 2, a, b, 2 * e + r % 2)
    )

    parts = rotate(at, every, 0, both_cores(act_shifts), 1)
    grad_square, parts = lax.optimization_barrier((grad_square, parts))
    grad_block = to_all(to_all(grad_square, ("zh",), 4), ("zl",), 4).reshape(16, 128, 256)
    parts = [move(parts[k], ("xh", "xl"), lambda a, p, k=k: (p ^ k, a)) for k in range(2)]
    rotated_act = parts[0] + parts[1]
    act_square = (rotated_act * rotated_act).astype(jnp.bfloat16)
    acts = both_cores(shifts(act_square))

    theirs = swap(correct(jnp.stack([y, c, 1 - turned]), acts, grad_block), "xl")
    mine = correct(at, acts, grad_block)
    return (mine + theirs) * (1.0 / tokens)


def solution(mesh):
    fine = Mesh(mesh.devices.reshape(SIZES), AXES)
    spec = P(("xh", "y", "c"), ("xl", "zh", "zl"))
    return jax.shard_map(
        on_device,
        mesh=fine,
        in_specs=(spec, spec, spec, spec),
        out_specs=P(("xl", "zh", "zl"), ("xh", "y", "c")),
        check_vma=False,
    )
```

```python
import functools
import jax
import jax.numpy as jnp
from jax import lax
from jax.experimental import pallas as pl
from jax.experimental.pallas import tpu as pltpu
from jax.sharding import Mesh, PartitionSpec as P

AXES = ("xh", "y", "c", "xl", "zh", "zl")
SIZES = (2, 4, 2, 2, 4, 4)
VMEM = pl.BlockSpec(memory_space=pltpu.VMEM)
SMEM = pl.BlockSpec(memory_space=pltpu.SMEM)
PARAMS = pltpu.CompilerParams(vmem_limit_bytes=40 * 1024 * 1024)


def to_all(x, axes, n):
    spread = jnp.broadcast_to(x[None], (n,) + x.shape)
    return lax.all_to_all(spread, axes, split_axis=0, concat_axis=0, tiled=True)


def move(x, axes, target):
    sizes = [SIZES[AXES.index(a)] for a in axes]

    def flat(coords):
        out = 0
        for c, s in zip(coords, sizes):
            out = out * s + c
        return out

    total = 1
    for s in sizes:
        total *= s
    pairs = []
    for i in range(total):
        rest, coords = i, []
        for s in reversed(sizes):
            coords.insert(0, rest % s)
            rest //= s
        pairs.append((i, flat(target(*coords))))
    return lax.ppermute(x, axes, pairs)


def dot(a, b):
    return jnp.dot(a, b, preferred_element_type=jnp.float32)


def rotate_kernel(at_ref, x_ref, own_ref, other_ref, first_ref, second_ref):
    y, c, turned = at_ref[0], at_ref[1], at_ref[2]
    sums = []
    for k in range(2):
        acc = jnp.zeros(x_ref.shape[2:], jnp.float32)
        for j in range(4):
            at = 4 * lax.rem(y + 4 - j, 4)
            for h in range(2):
                rows = slice(256 * h, 256 * h + 256)
                acc += dot(x_ref[at + 2 * c + h, 0], own_ref[j, k, rows, :])
                acc += dot(x_ref[at + 2 * (1 - c) + h, 0], other_ref[j, k, rows, :])
        sums.append(acc)
    near, far = sums
    mine, theirs = jnp.where(turned == 0, near, far), jnp.where(turned == 0, far, near)
    if len(first_ref.shape) == 2:
        first_ref[...], second_ref[...] = mine, theirs
    else:
        first_ref[0], first_ref[1] = mine, theirs
        second_ref[0], second_ref[1] = theirs, mine


def corrected_kernel(at_ref, own_ref, other_ref, s_ref, out_ref):
    y, c, k = at_ref[0], at_ref[1], at_ref[2]
    for h in range(2):
        acc = jnp.zeros((256, 256), jnp.float32)
        for j in range(4):
            at = lax.rem(y + 4 - j, 4) + 4 * h
            for act, core in ((own_ref, c), (other_ref, 1 - c)):
                acc += lax.dot_general(
                    act[j, k], s_ref[at + 8 * core],
                    (((0,), (0,)), ((), ())), preferred_element_type=jnp.float32,
                )
        out_ref[:, 256 * h:256 * h + 256] = acc


def rotate(at, x, part, basis, paired):
    out = jax.ShapeDtypeStruct((2,) * paired + x.shape[2:], jnp.float32)
    return pl.pallas_call(
        rotate_kernel,
        grid=(1,),
        out_shape=[out, out],
        in_specs=[SMEM, pl.BlockSpec((16, 1) + x.shape[2:], lambda i: (0, part, 0, 0)), VMEM, VMEM],
        out_specs=[VMEM, VMEM],
        compiler_params=PARAMS,
    )(at, x, *basis)


def correct(at, acts, grads):
    return pl.pallas_call(
        corrected_kernel,
        out_shape=jax.ShapeDtypeStruct((256, 512), jnp.float32),
        in_specs=[SMEM] + [VMEM] * 3,
        out_specs=VMEM,
        compiler_params=PARAMS,
    )(at, *acts, grads)


def swap(x, axis):
    return move(x, (axis,), lambda i: (1 - i,))


def cross(x):
    return jnp.stack([move(x, ("xh", "xl"), lambda a, p, k=k: (p ^ k, a)) for k in range(2)])


def shifts(pair):
    return [pair] + [move(pair, ("y",), lambda b, j=j: ((b + j) % 4,)) for j in (1, 2, 3)]


def both_cores(blocks):
    own = jnp.stack(blocks)
    return own, swap(own, "c")


def on_device(activations, gradients, act_basis, grad_basis):
    tokens = activations.shape[0] * 16
    xh, y, c, xl = (lax.axis_index(a) for a in ("xh", "y", "c", "xl"))
    turned = (xh + xl) % 2
    at = jnp.stack([y, c, turned])

    both = jnp.stack([activations, gradients])
    both, grad_basis = lax.optimization_barrier((both, grad_basis))
    every = lax.all_gather(both, ("zh", "zl"), axis=0, tiled=False)
    grad_pair = cross(grad_basis)
    act_basis, grad_pair = lax.optimization_barrier((act_basis, grad_pair))
    grad_shifts, act_pair = lax.optimization_barrier((shifts(grad_pair), cross(act_basis)))
    grad_panels = both_cores(grad_shifts)
    act_pair, grad_own = lax.optimization_barrier((act_pair, grad_panels[0]))
    act_shifts = shifts(act_pair)

    mine, theirs = rotate(at, every, 1, grad_panels, 0)
    rotated_grad = mine + swap(theirs, "xl")
    grad_square = (rotated_grad * rotated_grad).astype(jnp.bfloat16)
    act_shifts, grad_square = lax.optimization_barrier((act_shifts, grad_square))
    grad_square = move(
        grad_square, AXES, lambda a, b, e, p, q, r: (p, q, r // 2, a, b, 2 * e + r % 2)
    )

    parts = rotate(at, every, 0, both_cores(act_shifts), 1)
    grad_square, parts = lax.optimization_barrier((grad_square, parts))
    grad_block = to_all(grad_square, ("zh",), 4)
    parts = [move(parts[k], ("xh", "xl"), lambda a, p, k=k: (p ^ k, a)) for k in range(2)]
    rotated_act = parts[0] + parts[1]
    act_square = (rotated_act * rotated_act).astype(jnp.bfloat16)
    grad_block, act_square = lax.optimization_barrier((grad_block, act_square))
    grad_block = to_all(grad_block, ("zl",), 4).reshape(16, 128, 256)
    acts = both_cores(shifts(act_square))

    theirs = swap(correct(jnp.stack([y, c, 1 - turned]), acts, grad_block), "xl")
    mine = correct(at, acts, grad_block)
    return (mine + theirs) * (1.0 / tokens)


def solution(mesh):
    fine = Mesh(mesh.devices.reshape(SIZES), AXES)
    spec = P(("xh", "y", "c"), ("xl", "zh", "zl"))
    return jax.shard_map(
        on_device,
        mesh=fine,
        in_specs=(spec, spec, spec, spec),
        out_specs=P(("xl", "zh", "zl"), ("xh", "y", "c")),
        check_vma=False,
    )
```

```python
import functools
import jax
import jax.numpy as jnp
from jax import lax
from jax.experimental import pallas as pl
from jax.experimental.pallas import tpu as pltpu
from jax.sharding import Mesh, PartitionSpec as P

AXES = ("xh", "y", "c", "xl", "zh", "zl")
SIZES = (2, 4, 2, 2, 4, 4)
VMEM = pl.BlockSpec(memory_space=pltpu.VMEM)
SMEM = pl.BlockSpec(memory_space=pltpu.SMEM)
PARAMS = pltpu.CompilerParams(vmem_limit_bytes=40 * 1024 * 1024)


def to_all(x, axes, n):
    spread = jnp.broadcast_to(x[None], (n,) + x.shape)
    return lax.all_to_all(spread, axes, split_axis=0, concat_axis=0, tiled=True)


def move(x, axes, target):
    sizes = [SIZES[AXES.index(a)] for a in axes]

    def flat(coords):
        out = 0
        for c, s in zip(coords, sizes):
            out = out * s + c
        return out

    total = 1
    for s in sizes:
        total *= s
    pairs = []
    for i in range(total):
        rest, coords = i, []
        for s in reversed(sizes):
            coords.insert(0, rest % s)
            rest //= s
        pairs.append((i, flat(target(*coords))))
    return lax.ppermute(x, axes, pairs)


def dot(a, b):
    return jnp.dot(a, b, preferred_element_type=jnp.float32)


def rotate_kernel(at_ref, x_ref, own_ref, other_ref, first_ref, second_ref):
    y, c, turned = at_ref[0], at_ref[1], at_ref[2]
    sums = []
    for k in range(2):
        acc = jnp.zeros(x_ref.shape[2:], jnp.float32)
        for j in range(4):
            at = 4 * lax.rem(y + 4 - j, 4)
            for h in range(2):
                rows = slice(256 * h, 256 * h + 256)
                acc += dot(x_ref[at + 2 * c + h, 0], own_ref[j, k, rows, :])
                acc += dot(x_ref[at + 2 * (1 - c) + h, 0], other_ref[j, k, rows, :])
        sums.append(acc)
    near, far = sums
    mine, theirs = jnp.where(turned == 0, near, far), jnp.where(turned == 0, far, near)
    if len(first_ref.shape) == 2:
        first_ref[...], second_ref[...] = mine, theirs
    else:
        first_ref[0], first_ref[1] = mine, theirs
        second_ref[0], second_ref[1] = theirs, mine


def corrected_kernel(at_ref, own_ref, other_ref, s_ref, out_ref):
    y, c, k, zh = at_ref[0], at_ref[1], at_ref[2], at_ref[3]
    for h in range(2):
        acc = jnp.zeros((256, 256), jnp.float32)
        for j in range(4):
            at = lax.rem(zh + 4 - y + j, 4) + 4 * h
            for act, core in ((own_ref, c), (other_ref, 1 - c)):
                acc += lax.dot_general(
                    act[j, k], s_ref[at + 8 * core],
                    (((0,), (0,)), ((), ())), preferred_element_type=jnp.float32,
                )
        out_ref[:, 256 * h:256 * h + 256] = acc


def rotate(at, x, part, basis, paired):
    out = jax.ShapeDtypeStruct((2,) * paired + x.shape[2:], jnp.float32)
    return pl.pallas_call(
        rotate_kernel,
        grid=(1,),
        out_shape=[out, out],
        in_specs=[SMEM, pl.BlockSpec((16, 1) + x.shape[2:], lambda i: (0, part, 0, 0)), VMEM, VMEM],
        out_specs=[VMEM, VMEM],
        compiler_params=PARAMS,
    )(at, x, *basis)


def correct(at, acts, grads):
    return pl.pallas_call(
        corrected_kernel,
        out_shape=jax.ShapeDtypeStruct((256, 512), jnp.float32),
        in_specs=[SMEM] + [VMEM] * 3,
        out_specs=VMEM,
        compiler_params=PARAMS,
    )(at, *acts, grads)


def swap(x, axis):
    return move(x, (axis,), lambda i: (1 - i,))


def cross(x):
    return jnp.stack([move(x, ("xh", "xl"), lambda a, p, k=k: (p ^ k, a)) for k in range(2)])


def shifts(pair):
    return [pair] + [move(pair, ("y",), lambda b, j=j: ((b + j) % 4,)) for j in (1, 2, 3)]


def both_cores(blocks):
    own = jnp.stack(blocks)
    return own, swap(own, "c")


def on_device(activations, gradients, act_basis, grad_basis):
    tokens = activations.shape[0] * 16
    xh, y, c, xl, zh = (lax.axis_index(a) for a in AXES[:5])
    turned = (xh + xl) % 2
    at = jnp.stack([y, c, turned])

    both = jnp.stack([activations, gradients])
    both, grad_basis = lax.optimization_barrier((both, grad_basis))
    every = lax.all_gather(both, ("zh", "zl"), axis=0, tiled=False)
    grad_pair = cross(grad_basis)
    act_basis, grad_pair = lax.optimization_barrier((act_basis, grad_pair))
    grad_shifts, act_pair = lax.optimization_barrier((shifts(grad_pair), cross(act_basis)))
    grad_panels = both_cores(grad_shifts)
    act_pair, grad_own = lax.optimization_barrier((act_pair, grad_panels[0]))
    act_shifts = shifts(act_pair)

    mine, theirs = rotate(at, every, 1, grad_panels, 0)
    act_shifts, mine = lax.optimization_barrier((act_shifts, mine))
    act_own = jnp.stack(act_shifts)
    theirs, act_own = lax.optimization_barrier((swap(theirs, "xl"), act_own))
    rotated_grad = mine + theirs
    grad_square = (rotated_grad * rotated_grad).astype(jnp.bfloat16)
    grad_block = jnp.stack([
        move(
            grad_square, AXES,
            lambda a, b, e, p, q, r, k=k: (p, q, r // 2, a, (b + k) % 4, 2 * e + r % 2),
        )
        for k in range(4)
    ])

    parts = rotate(at, every, 0, (act_own, swap(act_own, "c")), 1)
    parts = [move(parts[k], ("xh", "xl"), lambda a, p, k=k: (p ^ k, a)) for k in range(2)]
    rotated_act = parts[0] + parts[1]
    act_square = (rotated_act * rotated_act).astype(jnp.bfloat16)
    grad_block, act_square = lax.optimization_barrier((grad_block, act_square))
    grad_block = to_all(grad_block, ("zl",), 4).reshape(16, 128, 256)
    acts = both_cores(shifts(act_square))

    theirs = swap(correct(jnp.stack([y, c, 1 - turned, zh]), acts, grad_block), "xl")
    mine = correct(jnp.stack([y, c, turned, zh]), acts, grad_block)
    return (mine + theirs) * (1.0 / tokens)


def solution(mesh):
    fine = Mesh(mesh.devices.reshape(SIZES), AXES)
    spec = P(("xh", "y", "c"), ("xl", "zh", "zl"))
    return jax.shard_map(
        on_device,
        mesh=fine,
        in_specs=(spec, spec, spec, spec),
        out_specs=P(("xl", "zh", "zl"), ("xh", "y", "c")),
        check_vma=False,
    )
```

```python
import functools
import jax
import jax.numpy as jnp
from jax import lax
from jax.experimental import pallas as pl
from jax.experimental.pallas import tpu as pltpu
from jax.sharding import Mesh, PartitionSpec as P

AXES = ("xh", "y", "c", "xl", "zh", "zl")
SIZES = (2, 4, 2, 2, 4, 4)
VMEM = pl.BlockSpec(memory_space=pltpu.VMEM)
HBM = pl.BlockSpec(memory_space=pltpu.HBM)
SMEM = pl.BlockSpec(memory_space=pltpu.SMEM)
PARAMS = pltpu.CompilerParams(vmem_limit_bytes=40 * 1024 * 1024)


def to_all(x, axes, n):
    spread = jnp.broadcast_to(x[None], (n,) + x.shape)
    return lax.all_to_all(spread, axes, split_axis=0, concat_axis=0, tiled=True)


def move(x, axes, target):
    sizes = [SIZES[AXES.index(a)] for a in axes]

    def flat(coords):
        out = 0
        for c, s in zip(coords, sizes):
            out = out * s + c
        return out

    total = 1
    for s in sizes:
        total *= s
    pairs = []
    for i in range(total):
        rest, coords = i, []
        for s in reversed(sizes):
            coords.insert(0, rest % s)
            rest //= s
        pairs.append((i, flat(target(*coords))))
    return lax.ppermute(x, axes, pairs)


def dot(a, b):
    return jnp.dot(a, b, preferred_element_type=jnp.float32)


def rotate_kernel(part, at_ref, x_hbm, own_ref, other_hbm, first_ref, second_ref, x_ref, other_ref, sems):
    copies = [
        pltpu.make_async_copy(x_hbm.at[:, part], x_ref, sems.at[0]),
        pltpu.make_async_copy(other_hbm, other_ref, sems.at[1]),
    ]
    for copy in copies:
        copy.start()
    y, c, turned = at_ref[0], at_ref[1], at_ref[2]
    sums = [jnp.zeros(x_ref.shape[1:], jnp.float32)] * 2
    for copy, basis, core in ((copies[0], own_ref, c), (copies[1], other_ref, 1 - c)):
        copy.wait()
        for k in range(2):
            for j in range(4):
                at = 4 * lax.rem(y + 4 - j, 4) + 2 * core
                for h in range(2):
                    sums[k] += dot(x_ref[at + h], basis[j, k, 256 * h:256 * h + 256, :])
    near, far = sums
    mine, theirs = jnp.where(turned == 0, near, far), jnp.where(turned == 0, far, near)
    if len(first_ref.shape) == 2:
        first_ref[...], second_ref[...] = mine, theirs
    else:
        first_ref[0], first_ref[1] = mine, theirs
        second_ref[0], second_ref[1] = theirs, mine


def corrected_kernel(at_ref, own_ref, other_ref, s_ref, out_ref):
    y, c, k = at_ref[0], at_ref[1], at_ref[2]
    for h in range(2):
        acc = jnp.zeros((256, 256), jnp.float32)
        for j in range(4):
            at = 4 * lax.rem(y + 4 - j, 4) + h
            for act, core in ((own_ref, c), (other_ref, 1 - c)):
                acc += lax.dot_general(
                    act[j, k], s_ref[at + 2 * core],
                    (((0,), (0,)), ((), ())), preferred_element_type=jnp.float32,
                )
        out_ref[:, 256 * h:256 * h + 256] = acc


def rotate(at, x, part, basis, paired):
    out = jax.ShapeDtypeStruct((2,) * paired + x.shape[2:], jnp.float32)
    own, other = basis
    x, other = (pltpu.with_memory_space_constraint(v, pltpu.HBM) for v in (x, other))
    return pl.pallas_call(
        functools.partial(rotate_kernel, part),
        out_shape=[out, out],
        in_specs=[SMEM, HBM, VMEM, HBM],
        out_specs=[VMEM, VMEM],
        scratch_shapes=[
            pltpu.VMEM((16,) + x.shape[2:], x.dtype),
            pltpu.VMEM(other.shape, other.dtype),
            pltpu.SemaphoreType.DMA((2,)),
        ],
        compiler_params=PARAMS,
    )(at, x, own, other)


def correct(at, acts, grads):
    return pl.pallas_call(
        corrected_kernel,
        out_shape=jax.ShapeDtypeStruct((256, 512), jnp.float32),
        in_specs=[SMEM] + [VMEM] * 3,
        out_specs=VMEM,
        compiler_params=PARAMS,
    )(at, *acts, grads)


def swap(x, axis):
    return move(x, (axis,), lambda i: (1 - i,))


def cross(x):
    return jnp.stack([move(x, ("xh", "xl"), lambda a, p, k=k: (p ^ k, a)) for k in range(2)])


def shifts(pair):
    return [pair] + [move(pair, ("y",), lambda b, j=j: ((b + j) % 4,)) for j in (1, 2, 3)]


def both_cores(blocks):
    own = jnp.stack(blocks)
    return own, swap(own, "c")


def on_device(activations, gradients, act_basis, grad_basis):
    tokens = activations.shape[0] * 16
    xh, y, c, xl = (lax.axis_index(a) for a in ("xh", "y", "c", "xl"))
    turned = (xh + xl) % 2
    at = jnp.stack([y, c, turned])

    both = jnp.stack([activations, gradients])
    both, grad_basis = lax.optimization_barrier((both, grad_basis))
    every = lax.all_gather(both, ("zh", "zl"), axis=0, tiled=False)
    grad_pair = cross(grad_basis)
    act_basis, grad_pair = lax.optimization_barrier((act_basis, grad_pair))
    grad_shifts, act_pair = lax.optimization_barrier((shifts(grad_pair), cross(act_basis)))
    grad_panels = both_cores(grad_shifts)
    act_pair, grad_own = lax.optimization_barrier((act_pair, grad_panels[0]))
    act_shifts = shifts(act_pair)

    mine, theirs = rotate(at, every, 1, grad_panels, 0)
    rotated_grad = mine + swap(theirs, "xl")
    grad_square = (rotated_grad * rotated_grad).astype(jnp.bfloat16)
    grad_square = move(
        grad_square, AXES, lambda a, b, e, p, q, r: (p, q, r // 2, a, b, 2 * e + r % 2)
    )
    act_shifts, grad_square = lax.optimization_barrier((act_shifts, grad_square))
    grad_block = to_all(grad_square, ("zh", "zl"), 16)

    parts = rotate(at, every, 0, both_cores(act_shifts), 1)
    parts = [move(parts[k], ("xh", "xl"), lambda a, p, k=k: (p ^ k, a)) for k in range(2)]
    rotated_act = parts[0] + parts[1]
    act_square = (rotated_act * rotated_act).astype(jnp.bfloat16)
    acts = both_cores(shifts(act_square))

    theirs = swap(correct(jnp.stack([y, c, 1 - turned]), acts, grad_block), "xl")
    mine = correct(at, acts, grad_block)
    return (mine + theirs) * (1.0 / tokens)


def solution(mesh):
    fine = Mesh(mesh.devices.reshape(SIZES), AXES)
    spec = P(("xh", "y", "c"), ("xl", "zh", "zl"))
    return jax.shard_map(
        on_device,
        mesh=fine,
        in_specs=(spec, spec, spec, spec),
        out_specs=P(("xl", "zh", "zl"), ("xh", "y", "c")),
        check_vma=False,
    )
```

```python
import functools
import jax
import jax.numpy as jnp
from jax import lax
from jax.experimental import pallas as pl
from jax.experimental.pallas import tpu as pltpu
from jax.sharding import Mesh, PartitionSpec as P

AXES = ("xh", "y", "c", "xl", "zh", "zl")
SIZES = (2, 4, 2, 2, 4, 4)
VMEM = pl.BlockSpec(memory_space=pltpu.VMEM)
HBM = pl.BlockSpec(memory_space=pltpu.HBM)
SMEM = pl.BlockSpec(memory_space=pltpu.SMEM)
PARAMS = pltpu.CompilerParams(vmem_limit_bytes=40 * 1024 * 1024)


def to_all(x, axes, n):
    spread = jnp.broadcast_to(x[None], (n,) + x.shape)
    return lax.all_to_all(spread, axes, split_axis=0, concat_axis=0, tiled=True)


def move(x, axes, target):
    sizes = [SIZES[AXES.index(a)] for a in axes]

    def flat(coords):
        out = 0
        for c, s in zip(coords, sizes):
            out = out * s + c
        return out

    total = 1
    for s in sizes:
        total *= s
    pairs = []
    for i in range(total):
        rest, coords = i, []
        for s in reversed(sizes):
            coords.insert(0, rest % s)
            rest //= s
        pairs.append((i, flat(target(*coords))))
    return lax.ppermute(x, axes, pairs)


def dot(a, b):
    return jnp.dot(a, b, preferred_element_type=jnp.float32)


def rotate_kernel(part, at_ref, x_hbm, own_ref, other_hbm, first_ref, second_ref, x_ref, sems, *held):
    copies = [pltpu.make_async_copy(x_hbm.at[:, part], x_ref, sems.at[0])]
    other_ref = held[0] if held else other_hbm
    if held:
        copies.append(pltpu.make_async_copy(other_hbm, other_ref, sems.at[1]))
    for copy in copies:
        copy.start()
    y, c, turned = at_ref[0], at_ref[1], at_ref[2]
    sums = [jnp.zeros(x_ref.shape[1:], jnp.float32)] * 2
    for half, basis, core in ((0, own_ref, c), (1, other_ref, 1 - c)):
        if half < len(copies):
            copies[half].wait()
        for k in range(2):
            for j in range(4):
                at = 4 * lax.rem(y + 4 - j, 4) + 2 * core
                for h in range(2):
                    sums[k] += dot(x_ref[at + h], basis[j, k, 256 * h:256 * h + 256, :])
    near, far = sums
    mine, theirs = jnp.where(turned == 0, near, far), jnp.where(turned == 0, far, near)
    if len(first_ref.shape) == 2:
        first_ref[...], second_ref[...] = mine, theirs
    else:
        first_ref[0], first_ref[1] = mine, theirs
        second_ref[0], second_ref[1] = theirs, mine


def corrected_kernel(at_ref, own_ref, other_ref, s_ref, out_ref):
    y, c, k = at_ref[0], at_ref[1], at_ref[2]
    for h in range(2):
        acc = jnp.zeros((256, 256), jnp.float32)
        for j in range(4):
            at = lax.rem(y + 4 - j, 4) + 4 * h
            for act, core in ((own_ref, c), (other_ref, 1 - c)):
                acc += lax.dot_general(
                    act[j, k], s_ref[at + 8 * core],
                    (((0,), (0,)), ((), ())), preferred_element_type=jnp.float32,
                )
        out_ref[:, 256 * h:256 * h + 256] = acc


def rotate(at, x, part, basis, paired):
    out = jax.ShapeDtypeStruct((2,) * paired + x.shape[2:], jnp.float32)
    own, other = basis
    x = pltpu.with_memory_space_constraint(x, pltpu.HBM)
    if not paired:
        other = pltpu.with_memory_space_constraint(other, pltpu.HBM)
    return pl.pallas_call(
        functools.partial(rotate_kernel, part),
        out_shape=[out, out],
        in_specs=[SMEM, HBM, VMEM, VMEM if paired else HBM],
        out_specs=[VMEM, VMEM],
        scratch_shapes=[
            pltpu.VMEM((16,) + x.shape[2:], x.dtype),
            pltpu.SemaphoreType.DMA((2,)),
        ] + [pltpu.VMEM(other.shape, other.dtype)] * (1 - paired),
        compiler_params=PARAMS,
    )(at, x, own, other)


def correct(at, acts, grads):
    return pl.pallas_call(
        corrected_kernel,
        out_shape=jax.ShapeDtypeStruct((256, 512), jnp.float32),
        in_specs=[SMEM] + [VMEM] * 3,
        out_specs=VMEM,
        compiler_params=PARAMS,
    )(at, *acts, grads)


def swap(x, axis):
    return move(x, (axis,), lambda i: (1 - i,))


def cross(x):
    return jnp.stack([move(x, ("xh", "xl"), lambda a, p, k=k: (p ^ k, a)) for k in range(2)])


def shifts(pair):
    return [pair] + [move(pair, ("y",), lambda b, j=j: ((b + j) % 4,)) for j in (1, 2, 3)]


def both_cores(blocks):
    own = jnp.stack(blocks)
    return own, swap(own, "c")


def on_device(activations, gradients, act_basis, grad_basis):
    tokens = activations.shape[0] * 16
    xh, y, c, xl = (lax.axis_index(a) for a in ("xh", "y", "c", "xl"))
    turned = (xh + xl) % 2
    at = jnp.stack([y, c, turned])

    both = jnp.stack([activations, gradients])
    both, grad_basis = lax.optimization_barrier((both, grad_basis))
    every = lax.all_gather(both, ("zh", "zl"), axis=0, tiled=False)
    grad_pair = cross(grad_basis)
    act_basis, grad_pair = lax.optimization_barrier((act_basis, grad_pair))
    grad_panels = both_cores(shifts(grad_pair))
    act_shifts, grad_own = lax.optimization_barrier((shifts(cross(act_basis)), grad_panels[0]))
    grad_panels = (grad_own, grad_panels[1])

    mine, theirs = rotate(at, every, 1, grad_panels, 0)
    rotated_grad = mine + swap(theirs, "xl")
    grad_square = (rotated_grad * rotated_grad).astype(jnp.bfloat16)
    grad_square = move(
        grad_square, AXES, lambda a, b, e, p, q, r: (p, q, r // 2, a, b, 2 * e + r % 2)
    )

    parts = rotate(at, every, 0, both_cores(act_shifts), 1)
    grad_square, parts = lax.optimization_barrier((grad_square, parts))
    grad_block = to_all(grad_square, ("zh",), 4)
    parts = [move(parts[k], ("xh", "xl"), lambda a, p, k=k: (p ^ k, a)) for k in range(2)]
    rotated_act = parts[0] + parts[1]
    act_square = (rotated_act * rotated_act).astype(jnp.bfloat16)
    grad_block, act_square = lax.optimization_barrier((grad_block, act_square))
    grad_block = to_all(grad_block, ("zl",), 4).reshape(16, 128, 256)
    acts = both_cores(shifts(act_square))

    theirs = swap(correct(jnp.stack([y, c, 1 - turned]), acts, grad_block), "xl")
    mine = correct(at, acts, grad_block)
    return (mine + theirs) * (1.0 / tokens)


def solution(mesh):
    fine = Mesh(mesh.devices.reshape(SIZES), AXES)
    spec = P(("xh", "y", "c"), ("xl", "zh", "zl"))
    return jax.shard_map(
        on_device,
        mesh=fine,
        in_specs=(spec, spec, spec, spec),
        out_specs=P(("xl", "zh", "zl"), ("xh", "y", "c")),
        check_vma=False,
    )
```

```python
import functools
import jax
import jax.numpy as jnp
from jax import lax
from jax.experimental import pallas as pl
from jax.experimental.pallas import tpu as pltpu
from jax.sharding import Mesh, PartitionSpec as P

AXES = ("xh", "y", "c", "xl", "zh", "zl")
SIZES = (2, 4, 2, 2, 4, 4)
VMEM = pl.BlockSpec(memory_space=pltpu.VMEM)
HBM = pl.BlockSpec(memory_space=pltpu.HBM)
SMEM = pl.BlockSpec(memory_space=pltpu.SMEM)
PARAMS = pltpu.CompilerParams(vmem_limit_bytes=40 * 1024 * 1024)


def to_all(x, axes, n):
    spread = jnp.broadcast_to(x[None], (n,) + x.shape)
    return lax.all_to_all(spread, axes, split_axis=0, concat_axis=0, tiled=True)


def move(x, axes, target):
    sizes = [SIZES[AXES.index(a)] for a in axes]

    def flat(coords):
        out = 0
        for c, s in zip(coords, sizes):
            out = out * s + c
        return out

    total = 1
    for s in sizes:
        total *= s
    pairs = []
    for i in range(total):
        rest, coords = i, []
        for s in reversed(sizes):
            coords.insert(0, rest % s)
            rest //= s
        pairs.append((i, flat(target(*coords))))
    return lax.ppermute(x, axes, pairs)


def dot(a, b):
    return jnp.dot(a, b, preferred_element_type=jnp.float32)


def rotate_kernel(part, at_ref, x_hbm, own_ref, other_hbm, first_ref, second_ref, x_ref, sems, *held):
    copies = [pltpu.make_async_copy(x_hbm.at[:, part], x_ref, sems.at[0])]
    other_ref = held[0] if held else other_hbm
    if held:
        copies.append(pltpu.make_async_copy(other_hbm, other_ref, sems.at[1]))
    for copy in copies:
        copy.start()
    y, c, turned = at_ref[0], at_ref[1], at_ref[2]
    sums = [jnp.zeros(x_ref.shape[1:], jnp.float32)] * 2
    for half, basis, core in ((0, own_ref, c), (1, other_ref, 1 - c)):
        if half < len(copies):
            copies[half].wait()
        for k in range(2):
            for j in range(4):
                at = 4 * lax.rem(y + 4 - j, 4) + 2 * core
                for h in range(2):
                    sums[k] += dot(x_ref[at + h], basis[j, k, 256 * h:256 * h + 256, :])
    near, far = sums
    mine, theirs = jnp.where(turned == 0, near, far), jnp.where(turned == 0, far, near)
    if len(first_ref.shape) == 2:
        first_ref[...], second_ref[...] = mine, theirs
    else:
        first_ref[0], first_ref[1] = mine, theirs
        second_ref[0], second_ref[1] = theirs, mine


def corrected_kernel(at_ref, own_ref, other_ref, s_ref, out_ref):
    y, c, k = at_ref[0], at_ref[1], at_ref[2]
    for h in range(2):
        acc = jnp.zeros((256, 128), jnp.float32)
        for j in range(4):
            at = 4 * lax.rem(y + 4 - j, 4) + h
            for act, core in ((own_ref, c), (other_ref, 1 - c)):
                acc += lax.dot_general(
                    act[j, k], s_ref[at + 2 * core],
                    (((0,), (0,)), ((), ())), preferred_element_type=jnp.float32,
                )
        out_ref[:, 128 * h:128 * h + 128] = acc


def rotate(at, x, part, basis, paired):
    out = jax.ShapeDtypeStruct((2,) * paired + x.shape[2:], jnp.float32)
    own, other = basis
    x = pltpu.with_memory_space_constraint(x, pltpu.HBM)
    if not paired:
        other = pltpu.with_memory_space_constraint(other, pltpu.HBM)
    return pl.pallas_call(
        functools.partial(rotate_kernel, part),
        out_shape=[out, out],
        in_specs=[SMEM, HBM, VMEM, VMEM if paired else HBM],
        out_specs=[VMEM, VMEM],
        scratch_shapes=[
            pltpu.VMEM((16,) + x.shape[2:], x.dtype),
            pltpu.SemaphoreType.DMA((2,)),
        ] + [pltpu.VMEM(other.shape, other.dtype)] * (1 - paired),
        compiler_params=PARAMS,
    )(at, x, own, other)


def correct(at, acts, grads):
    return pl.pallas_call(
        corrected_kernel,
        out_shape=jax.ShapeDtypeStruct((256, 256), jnp.float32),
        in_specs=[SMEM] + [VMEM] * 3,
        out_specs=VMEM,
        compiler_params=PARAMS,
    )(at, *acts, grads)


def swap(x, axis):
    return move(x, (axis,), lambda i: (1 - i,))


def cross(x):
    return jnp.stack([move(x, ("xh", "xl"), lambda a, p, k=k: (p ^ k, a)) for k in range(2)])


def shifts(pair):
    return [pair] + [move(pair, ("y",), lambda b, j=j: ((b + j) % 4,)) for j in (1, 2, 3)]


def both_cores(blocks):
    own = jnp.stack(blocks)
    return own, swap(own, "c")


def on_device(activations, gradients, act_basis, grad_basis):
    tokens = activations.shape[0] * 16
    xh, y, c, xl = (lax.axis_index(a) for a in ("xh", "y", "c", "xl"))
    turned = (xh + xl) % 2
    at = jnp.stack([y, c, turned])

    both = jnp.stack([activations, gradients])
    both, grad_basis = lax.optimization_barrier((both, grad_basis))
    every = lax.all_gather(both, ("zh", "zl"), axis=0, tiled=False)
    grad_pair = cross(grad_basis)
    act_basis, grad_pair = lax.optimization_barrier((act_basis, grad_pair))
    grad_shifts, act_pair = lax.optimization_barrier((shifts(grad_pair), cross(act_basis)))
    grad_panels = both_cores(grad_shifts)
    act_pair, grad_own = lax.optimization_barrier((act_pair, grad_panels[0]))
    act_shifts = shifts(act_pair)

    mine, theirs = rotate(at, every, 1, grad_panels, 0)
    rotated_grad = mine + swap(theirs, "xl")
    grad_square = (rotated_grad * rotated_grad).astype(jnp.bfloat16)
    act_shifts, grad_square = lax.optimization_barrier((act_shifts, grad_square))
    grad_square = move(
        grad_square, AXES, lambda a, b, e, p, q, r: (p, q, r // 2, a, b, 2 * e + r % 2)
    )

    parts = rotate(at, every, 0, both_cores(act_shifts), 1)
    grad_square, parts = lax.optimization_barrier((grad_square, parts))
    first = to_all(grad_square[:, :128], ("zh", "zl"), 16)
    parts = [move(parts[k], ("xh", "xl"), lambda a, p, k=k: (p ^ k, a)) for k in range(2)]
    rotated_act = parts[0] + parts[1]
    act_square = (rotated_act * rotated_act).astype(jnp.bfloat16)
    second, act_square = lax.optimization_barrier((grad_square[:, 128:], act_square))
    second = to_all(second, ("zh", "zl"), 16)
    acts = both_cores(shifts(act_square))

    halves = []
    for grads in (first, second):
        theirs = swap(correct(jnp.stack([y, c, 1 - turned]), acts, grads), "xl")
        halves.append((correct(at, acts, grads) + theirs) * (1.0 / tokens))
    low, high = halves
    return jnp.concatenate([low[:, :128], high[:, :128], low[:, 128:], high[:, 128:]], axis=1)


def solution(mesh):
    fine = Mesh(mesh.devices.reshape(SIZES), AXES)
    spec = P(("xh", "y", "c"), ("xl", "zh", "zl"))
    return jax.shard_map(
        on_device,
        mesh=fine,
        in_specs=(spec, spec, spec, spec),
        out_specs=P(("xl", "zh", "zl"), ("xh", "y", "c")),
        check_vma=False,
    )
```

```python
import functools
import jax
import jax.numpy as jnp
from jax import lax
from jax.experimental import pallas as pl
from jax.experimental.pallas import tpu as pltpu
from jax.sharding import Mesh, PartitionSpec as P

AXES = ("xh", "y", "c", "xl", "zh", "zl")
SIZES = (2, 4, 2, 2, 4, 4)
VMEM = pl.BlockSpec(memory_space=pltpu.VMEM)
HBM = pl.BlockSpec(memory_space=pltpu.HBM)
SMEM = pl.BlockSpec(memory_space=pltpu.SMEM)
PARAMS = pltpu.CompilerParams(vmem_limit_bytes=40 * 1024 * 1024)


def to_all(x, axes, n):
    spread = jnp.broadcast_to(x[None], (n,) + x.shape)
    return lax.all_to_all(spread, axes, split_axis=0, concat_axis=0, tiled=True)


def move(x, axes, target):
    sizes = [SIZES[AXES.index(a)] for a in axes]

    def flat(coords):
        out = 0
        for c, s in zip(coords, sizes):
            out = out * s + c
        return out

    total = 1
    for s in sizes:
        total *= s
    pairs = []
    for i in range(total):
        rest, coords = i, []
        for s in reversed(sizes):
            coords.insert(0, rest % s)
            rest //= s
        pairs.append((i, flat(target(*coords))))
    return lax.ppermute(x, axes, pairs)


def dot(a, b):
    return jnp.dot(a, b, preferred_element_type=jnp.float32)


def rotate_kernel(part, at_ref, x_hbm, own_ref, other_hbm, first_ref, second_ref, x_ref, sems, *held):
    copies = [pltpu.make_async_copy(x_hbm.at[:, part], x_ref, sems.at[0])]
    other_ref = held[0] if held else other_hbm
    if held:
        copies.append(pltpu.make_async_copy(other_hbm, other_ref, sems.at[1]))
    for copy in copies:
        copy.start()
    y, c, turned = at_ref[0], at_ref[1], at_ref[2]
    sums = [jnp.zeros(x_ref.shape[1:], jnp.float32)] * 2
    for half, basis, core in ((0, own_ref, c), (1, other_ref, 1 - c)):
        if half < len(copies):
            copies[half].wait()
        for k in range(2):
            for j in range(4):
                at = 4 * lax.rem(y + 4 - j, 4) + 2 * core
                for h in range(2):
                    sums[k] += dot(x_ref[at + h], basis[j, k, 256 * h:256 * h + 256, :])
    near, far = sums
    mine, theirs = jnp.where(turned == 0, near, far), jnp.where(turned == 0, far, near)
    if len(first_ref.shape) == 2:
        first_ref[...], second_ref[...] = mine, theirs
    else:
        first_ref[0], first_ref[1] = mine, theirs
        second_ref[0], second_ref[1] = theirs, mine


def corrected_kernel(at_ref, own_ref, other_ref, s_ref, out_ref):
    y, c, k = at_ref[0], at_ref[1], at_ref[2]
    for h in range(2):
        acc = jnp.zeros((256, 256), jnp.float32)
        for j in range(4):
            at = lax.rem(y + 4 - j, 4) + 4 * h
            for act, core in ((own_ref, c), (other_ref, 1 - c)):
                acc += lax.dot_general(
                    act[j, k], s_ref[at + 8 * core],
                    (((0,), (0,)), ((), ())), preferred_element_type=jnp.float32,
                )
        out_ref[:, 256 * h:256 * h + 256] = acc


def rotate(at, x, part, basis, paired):
    out = jax.ShapeDtypeStruct((2,) * paired + x.shape[2:], jnp.float32)
    own, other = basis
    x = pltpu.with_memory_space_constraint(x, pltpu.HBM)
    if not paired:
        other = pltpu.with_memory_space_constraint(other, pltpu.HBM)
    return pl.pallas_call(
        functools.partial(rotate_kernel, part),
        out_shape=[out, out],
        in_specs=[SMEM, HBM, VMEM, VMEM if paired else HBM],
        out_specs=[VMEM, VMEM],
        scratch_shapes=[
            pltpu.VMEM((16,) + x.shape[2:], x.dtype),
            pltpu.SemaphoreType.DMA((2,)),
        ] + [pltpu.VMEM(other.shape, other.dtype)] * (1 - paired),
        compiler_params=PARAMS,
    )(at, x, own, other)


def correct(at, acts, grads):
    return pl.pallas_call(
        corrected_kernel,
        out_shape=jax.ShapeDtypeStruct((256, 512), jnp.float32),
        in_specs=[SMEM] + [VMEM] * 3,
        out_specs=VMEM,
        compiler_params=PARAMS,
    )(at, *acts, grads)


def swap(x, axis):
    return move(x, (axis,), lambda i: (1 - i,))


def cross(x):
    return jnp.stack([move(x, ("xh", "xl"), lambda a, p, k=k: (p ^ k, a)) for k in range(2)])


def shifts(pair):
    return [pair] + [move(pair, ("y",), lambda b, j=j: ((b + j) % 4,)) for j in (1, 2, 3)]


def both_cores(blocks):
    own = jnp.stack(blocks)
    return own, swap(own, "c")


def on_device(activations, gradients, act_basis, grad_basis):
    tokens = activations.shape[0] * 16
    xh, y, c, xl = (lax.axis_index(a) for a in ("xh", "y", "c", "xl"))
    turned = (xh + xl) % 2
    at = jnp.stack([y, c, turned])

    both = jnp.stack([activations, gradients])
    both, grad_basis = lax.optimization_barrier((both, grad_basis))
    every = lax.all_gather(both, ("zh", "zl"), axis=0, tiled=False)
    grad_pair = cross(grad_basis)
    act_basis, grad_pair = lax.optimization_barrier((act_basis, grad_pair))
    grad_shifts, act_pair = lax.optimization_barrier((shifts(grad_pair), cross(act_basis)))
    grad_panels = both_cores(grad_shifts)
    act_pair, grad_own = lax.optimization_barrier((act_pair, grad_panels[0]))
    act_shifts = shifts(act_pair)

    mine, theirs = rotate(at, every, 1, grad_panels, 0)
    rotated_grad = mine + swap(theirs, "xl")
    grad_square = (rotated_grad * rotated_grad).astype(jnp.bfloat16)
    grad_square = move(
        grad_square, AXES, lambda a, b, e, p, q, r: (p, q, r // 2, a, b, 2 * e + r % 2)
    )
    act_shifts, grad_square = lax.optimization_barrier((act_shifts, grad_square))
    grad_block = to_all(grad_square, ("zh",), 4)

    parts = rotate(at, every, 0, both_cores(act_shifts), 1)
    parts = [move(parts[k], ("xh", "xl"), lambda a, p, k=k: (p ^ k, a)) for k in range(2)]
    rotated_act = parts[0] + parts[1]
    act_square = (rotated_act * rotated_act).astype(jnp.bfloat16)
    grad_block, act_square = lax.optimization_barrier((grad_block, act_square))
    grad_block = to_all(grad_block, ("zl",), 4).reshape(16, 128, 256)
    acts = both_cores(shifts(act_square))

    theirs = swap(correct(jnp.stack([y, c, 1 - turned]), acts, grad_block), "xl")
    mine = correct(at, acts, grad_block)
    return (mine + theirs) * (1.0 / tokens)


def solution(mesh):
    fine = Mesh(mesh.devices.reshape(SIZES), AXES)
    spec = P(("xh", "y", "c"), ("xl", "zh", "zl"))
    return jax.shard_map(
        on_device,
        mesh=fine,
        in_specs=(spec, spec, spec, spec),
        out_specs=P(("xl", "zh", "zl"), ("xh", "y", "c")),
        check_vma=False,
    )
```

```python
import functools
import jax
import jax.numpy as jnp
from jax import lax
from jax.experimental import pallas as pl
from jax.experimental.pallas import tpu as pltpu
from jax.sharding import Mesh, PartitionSpec as P

AXES = ("xh", "y", "c", "xl", "zh", "zl")
SIZES = (2, 4, 2, 2, 4, 4)
VMEM = pl.BlockSpec(memory_space=pltpu.VMEM)
HBM = pl.BlockSpec(memory_space=pltpu.HBM)
SMEM = pl.BlockSpec(memory_space=pltpu.SMEM)
PARAMS = pltpu.CompilerParams(vmem_limit_bytes=40 * 1024 * 1024)


def to_all(x, axes, n):
    spread = jnp.broadcast_to(x[None], (n,) + x.shape)
    return lax.all_to_all(spread, axes, split_axis=0, concat_axis=0, tiled=True)


def move(x, axes, target):
    sizes = [SIZES[AXES.index(a)] for a in axes]

    def flat(coords):
        out = 0
        for c, s in zip(coords, sizes):
            out = out * s + c
        return out

    total = 1
    for s in sizes:
        total *= s
    pairs = []
    for i in range(total):
        rest, coords = i, []
        for s in reversed(sizes):
            coords.insert(0, rest % s)
            rest //= s
        pairs.append((i, flat(target(*coords))))
    return lax.ppermute(x, axes, pairs)


def dot(a, b):
    return jnp.dot(a, b, preferred_element_type=jnp.float32)


def rotate_kernel(part, at_ref, x_hbm, own_ref, other_hbm, first_ref, second_ref, x_ref, sems, *held):
    copies = [pltpu.make_async_copy(x_hbm.at[:, part], x_ref, sems.at[0])]
    other_ref = held[0] if held else other_hbm
    if held:
        copies.append(pltpu.make_async_copy(other_hbm, other_ref, sems.at[1]))
    for copy in copies:
        copy.start()
    y, c, turned = at_ref[0], at_ref[1], at_ref[2]
    sums = [jnp.zeros(x_ref.shape[1:], jnp.float32)] * 2
    for half, basis, core in ((0, own_ref, c), (1, other_ref, 1 - c)):
        if half < len(copies):
            copies[half].wait()
        for k in range(2):
            for j in range(4):
                at = 4 * lax.rem(y + 4 - j, 4) + 2 * core
                for h in range(2):
                    sums[k] += dot(x_ref[at + h], basis[j, k, 256 * h:256 * h + 256, :])
    near, far = sums
    mine, theirs = jnp.where(turned == 0, near, far), jnp.where(turned == 0, far, near)
    if len(first_ref.shape) == 2:
        first_ref[...], second_ref[...] = mine, theirs
    else:
        first_ref[0], first_ref[1] = mine, theirs
        second_ref[0], second_ref[1] = theirs, mine


def corrected_kernel(at_ref, own_ref, other_ref, s_ref, out_ref):
    y, c, k = at_ref[0], at_ref[1], at_ref[2]
    for h in range(2):
        acc = jnp.zeros((256, 256), jnp.float32)
        for j in range(4):
            at = 4 * lax.rem(y + 4 - j, 4) + h
            for act, core in ((own_ref, c), (other_ref, 1 - c)):
                acc += lax.dot_general(
                    act[j, k], s_ref[at + 2 * core],
                    (((0,), (0,)), ((), ())), preferred_element_type=jnp.float32,
                )
        out_ref[:, 256 * h:256 * h + 256] = acc


def rotate(at, x, part, basis, paired):
    out = jax.ShapeDtypeStruct((2,) * paired + x.shape[2:], jnp.float32)
    own, other = basis
    x = pltpu.with_memory_space_constraint(x, pltpu.HBM)
    if not paired:
        other = pltpu.with_memory_space_constraint(other, pltpu.HBM)
    return pl.pallas_call(
        functools.partial(rotate_kernel, part),
        out_shape=[out, out],
        in_specs=[SMEM, HBM, VMEM, VMEM if paired else HBM],
        out_specs=[VMEM, VMEM],
        scratch_shapes=[
            pltpu.VMEM((16,) + x.shape[2:], x.dtype),
            pltpu.SemaphoreType.DMA((2,)),
        ] + [pltpu.VMEM(other.shape, other.dtype)] * (1 - paired),
        compiler_params=PARAMS,
    )(at, x, own, other)


def correct(at, acts, grads):
    return pl.pallas_call(
        corrected_kernel,
        out_shape=jax.ShapeDtypeStruct((256, 512), jnp.float32),
        in_specs=[SMEM] + [VMEM] * 3,
        out_specs=VMEM,
        compiler_params=PARAMS,
    )(at, *acts, grads)


def swap(x, axis):
    return move(x, (axis,), lambda i: (1 - i,))


def cross(x):
    return jnp.stack([move(x, ("xh", "xl"), lambda a, p, k=k: (p ^ k, a)) for k in range(2)])


def shifts(pair):
    return [pair] + [move(pair, ("y",), lambda b, j=j: ((b + j) % 4,)) for j in (1, 2, 3)]


def both_cores(blocks):
    own = jnp.stack(blocks)
    return own, swap(own, "c")


def on_device(activations, gradients, act_basis, grad_basis):
    tokens = activations.shape[0] * 16
    xh, y, c, xl = (lax.axis_index(a) for a in ("xh", "y", "c", "xl"))
    turned = (xh + xl) % 2
    at = jnp.stack([y, c, turned])

    both = jnp.stack([activations, gradients])
    both, grad_basis = lax.optimization_barrier((both, grad_basis))
    every = lax.all_gather(both, ("zh", "zl"), axis=0, tiled=False)
    grad_pair = cross(grad_basis)
    act_basis, grad_pair = lax.optimization_barrier((act_basis, grad_pair))
    grad_shifts, act_pair = lax.optimization_barrier((shifts(grad_pair), cross(act_basis)))
    grad_panels = both_cores(grad_shifts)
    act_pair, grad_own = lax.optimization_barrier((act_pair, grad_panels[0]))
    act_shifts = shifts(act_pair)

    mine, theirs = rotate(at, every, 1, grad_panels, 0)
    rotated_grad = mine + swap(theirs, "xl")
    grad_square = (rotated_grad * rotated_grad).astype(jnp.bfloat16)
    grad_square = move(
        grad_square, AXES, lambda a, b, e, p, q, r: (p, q, r // 2, a, b, 2 * e + r % 2)
    )
    act_shifts, grad_square = lax.optimization_barrier((act_shifts, grad_square))
    grad_block = to_all(grad_square, ("zh", "zl"), 16)

    parts = rotate(at, every, 0, both_cores(act_shifts), 1)
    parts = [move(parts[k], ("xh", "xl"), lambda a, p, k=k: (p ^ k, a)) for k in range(2)]
    rotated_act = parts[0] + parts[1]
    act_square = (rotated_act * rotated_act).astype(jnp.bfloat16)
    acts = both_cores(shifts(act_square))

    theirs = swap(correct(jnp.stack([y, c, 1 - turned]), acts, grad_block), "xl")
    mine = correct(at, acts, grad_block)
    return (mine + theirs) * (1.0 / tokens)


def solution(mesh):
    fine = Mesh(mesh.devices.reshape(SIZES), AXES)
    spec = P(("xh", "y", "c"), ("xl", "zh", "zl"))
    return jax.shard_map(
        on_device,
        mesh=fine,
        in_specs=(spec, spec, spec, spec),
        out_specs=P(("xl", "zh", "zl"), ("xh", "y", "c")),
        check_vma=False,
    )
```

```python
import functools
import jax
import jax.numpy as jnp
from jax import lax
from jax.experimental import pallas as pl
from jax.experimental.pallas import tpu as pltpu
from jax.sharding import Mesh, PartitionSpec as P

AXES = ("xh", "y", "c", "xl", "zh", "zl")
SIZES = (2, 4, 2, 2, 4, 4)
VMEM = pl.BlockSpec(memory_space=pltpu.VMEM)
HBM = pl.BlockSpec(memory_space=pltpu.HBM)
SMEM = pl.BlockSpec(memory_space=pltpu.SMEM)
PARAMS = pltpu.CompilerParams(vmem_limit_bytes=40 * 1024 * 1024)


def to_all(x, axes, n):
    spread = jnp.broadcast_to(x[None], (n,) + x.shape)
    return lax.all_to_all(spread, axes, split_axis=0, concat_axis=0, tiled=True)


def move(x, axes, target):
    sizes = [SIZES[AXES.index(a)] for a in axes]

    def flat(coords):
        out = 0
        for c, s in zip(coords, sizes):
            out = out * s + c
        return out

    total = 1
    for s in sizes:
        total *= s
    pairs = []
    for i in range(total):
        rest, coords = i, []
        for s in reversed(sizes):
            coords.insert(0, rest % s)
            rest //= s
        pairs.append((i, flat(target(*coords))))
    return lax.ppermute(x, axes, pairs)


def dot(a, b):
    return jnp.dot(a, b, preferred_element_type=jnp.float32)


def rotate_kernel(part, at_ref, x_hbm, own_ref, other_hbm, first_ref, second_ref, x_ref, sems, *held):
    copies = [pltpu.make_async_copy(x_hbm.at[:, part], x_ref, sems.at[0])]
    other_ref = held[0] if held else other_hbm
    if held:
        copies.append(pltpu.make_async_copy(other_hbm, other_ref, sems.at[1]))
    for copy in copies:
        copy.start()
    y, c, turned = at_ref[0], at_ref[1], at_ref[2]
    sums = [jnp.zeros(x_ref.shape[1:], jnp.float32)] * 2
    for half, basis, core in ((0, own_ref, c), (1, other_ref, 1 - c)):
        if half < len(copies):
            copies[half].wait()
        for k in range(2):
            for j in range(4):
                at = 4 * lax.rem(y + 4 - j, 4) + 2 * core
                for h in range(2):
                    sums[k] += dot(x_ref[at + h], basis[j, k, 256 * h:256 * h + 256, :])
    near, far = sums
    mine, theirs = jnp.where(turned == 0, near, far), jnp.where(turned == 0, far, near)
    if len(first_ref.shape) == 2:
        first_ref[...], second_ref[...] = mine, theirs
    else:
        first_ref[0], first_ref[1] = mine, theirs
        second_ref[0], second_ref[1] = theirs, mine


def corrected_kernel(at_ref, own_ref, other_ref, s_ref, out_ref):
    y, c, k = at_ref[0], at_ref[1], at_ref[2]
    for h in range(2):
        acc = jnp.zeros((256, 256), jnp.float32)
        for j in range(4):
            at = 4 * lax.rem(y + 4 - j, 4) + h
            for act, core in ((own_ref, c), (other_ref, 1 - c)):
                acc += lax.dot_general(
                    act[j, k], s_ref[at + 2 * core],
                    (((0,), (0,)), ((), ())), preferred_element_type=jnp.float32,
                )
        out_ref[:, 256 * h:256 * h + 256] = acc


def rotate(at, x, part, basis, paired):
    out = jax.ShapeDtypeStruct((2,) * paired + x.shape[2:], jnp.float32)
    own, other = basis
    x = pltpu.with_memory_space_constraint(x, pltpu.HBM)
    if not paired:
        other = pltpu.with_memory_space_constraint(other, pltpu.HBM)
    return pl.pallas_call(
        functools.partial(rotate_kernel, part),
        out_shape=[out, out],
        in_specs=[SMEM, HBM, VMEM, VMEM if paired else HBM],
        out_specs=[VMEM, VMEM],
        scratch_shapes=[
            pltpu.VMEM((16,) + x.shape[2:], x.dtype),
            pltpu.SemaphoreType.DMA((2,)),
        ] + [pltpu.VMEM(other.shape, other.dtype)] * (1 - paired),
        compiler_params=PARAMS,
    )(at, x, own, other)


def correct(at, acts, grads):
    return pl.pallas_call(
        corrected_kernel,
        out_shape=jax.ShapeDtypeStruct((256, 512), jnp.float32),
        in_specs=[SMEM] + [VMEM] * 3,
        out_specs=VMEM,
        compiler_params=PARAMS,
    )(at, *acts, grads)


def swap(x, axis):
    return move(x, (axis,), lambda i: (1 - i,))


def cross(x):
    return jnp.stack([move(x, ("xh", "xl"), lambda a, p, k=k: (p ^ k, a)) for k in range(2)])


def shifts(pair):
    return [pair] + [move(pair, ("y",), lambda b, j=j: ((b + j) % 4,)) for j in (1, 2, 3)]


def both_cores(blocks):
    own = jnp.stack(blocks)
    return own, swap(own, "c")


def on_device(activations, gradients, act_basis, grad_basis):
    tokens = activations.shape[0] * 16
    xh, y, c, xl = (lax.axis_index(a) for a in ("xh", "y", "c", "xl"))
    turned = (xh + xl) % 2
    at = jnp.stack([y, c, turned])

    both = jnp.stack([activations, gradients])
    both, grad_basis = lax.optimization_barrier((both, grad_basis))
    every = lax.all_gather(both, ("zh", "zl"), axis=0, tiled=False)
    grad_pair = cross(grad_basis)
    act_basis, grad_pair = lax.optimization_barrier((act_basis, grad_pair))
    grad_shifts, act_pair = lax.optimization_barrier((shifts(grad_pair), cross(act_basis)))
    grad_panels = both_cores(grad_shifts)
    act_shifts = shifts(act_pair)

    mine, theirs = rotate(at, every, 1, grad_panels, 0)
    rotated_grad = mine + swap(theirs, "xl")
    grad_square = (rotated_grad * rotated_grad).astype(jnp.bfloat16)
    grad_square = move(
        grad_square, AXES, lambda a, b, e, p, q, r: (p, q, r // 2, a, b, 2 * e + r % 2)
    )
    act_shifts, grad_square = lax.optimization_barrier((act_shifts, grad_square))
    grad_block = to_all(grad_square, ("zh", "zl"), 16)

    parts = rotate(at, every, 0, both_cores(act_shifts), 1)
    parts = [move(parts[k], ("xh", "xl"), lambda a, p, k=k: (p ^ k, a)) for k in range(2)]
    rotated_act = parts[0] + parts[1]
    act_square = (rotated_act * rotated_act).astype(jnp.bfloat16)
    acts = both_cores(shifts(act_square))

    theirs = swap(correct(jnp.stack([y, c, 1 - turned]), acts, grad_block), "xl")
    mine = correct(at, acts, grad_block)
    return (mine + theirs) * (1.0 / tokens)


def solution(mesh):
    fine = Mesh(mesh.devices.reshape(SIZES), AXES)
    spec = P(("xh", "y", "c"), ("xl", "zh", "zl"))
    return jax.shard_map(
        on_device,
        mesh=fine,
        in_specs=(spec, spec, spec, spec),
        out_specs=P(("xl", "zh", "zl"), ("xh", "y", "c")),
        check_vma=False,
    )
```
